256 devices in a mesh: section: 2 (over core), frame: 8 (over z_lo, y), tile: 16 (over x, z_hi).
Axes of the slice: x: 4, y: 4, z: 8 (z_hi: 4, z_lo: 2; z = z_hi * 2 + z_lo), core: 2. Of those that a mesh axis runs over, the one named last changes fastest.
Arguments:
- queries: bfloat16 [8, 16, 256, 1536], P('frame', 'tile', None, 'section'), may hold values from -5 to 5
- key_rows: bfloat16 [8, 16, 256, 1536], P('frame', 'tile', None, 'section'), may hold values from -5 to 5
- value_rows: bfloat16 [8, 16, 256, 1536], P('frame', 'tile', None, 'section'), may hold values from -6 to 6
- grad_rows: bfloat16 [8, 16, 256, 1536], P('frame', 'tile', 'section'), may hold values from -6 to 6
- offsets: int32 [12, 9, 3], P('section'), may hold values from -1 to 1, as said below
- counts: int32 [8, 16], replicated, may hold values from 8 to 256, as said below
Outputs:
- grad_query: bfloat16 [8, 16, 256, 1536], P('frame', 'tile', None, 'section')
- grad_key: bfloat16 [8, 16, 256, 1536], P('frame', 'tile', None, 'section')
- grad_value: bfloat16 [8, 16, 256, 1536], P('frame', 'tile', None, 'section')
The draws below stay inside these ranges and needn't reach their ends.
Inputs may be any that keep to these rules, and one draw needn't show every extreme that they name: `offsets`: of heads 2m and 2m + 1, one lists the nine tiles (0, a, b) and the other the nine tiles (a, b, 0), for a and b each of -1, 0, 1, each head in an order of its own. `counts`: the real tokens of a tile fill its first slots; tiles outside the last block of frames and the last row of spatial tiles are full; the last tile of the grid holds 8; a tile holds a multiple of 8 real tokens.
All inputs are finite; a program needn't handle non-finite values.
Results may differ from the reference program's by a relative error of at most 0.008.
Values may be sent and summed in bfloat16 or wider, within the bound.
A program may use at most 128 MiB of HBM per device.

```python
import math
import jax
import jax.numpy as jnp
from jax import lax

H = 12
HD = 128
D = 1536
TF = 4
TH = 8
TW = 8
TILE = 256
NCT = 4
NFT = 8
NST = 16


def draw_queries(key, part):
    sample = jnp.clip(jax.random.normal(jax.random.fold_in(key, 1), (NFT, NST, TILE, H * HD)), -4.0, 4.0)
    return sample.astype(jnp.bfloat16)


def draw_key_rows(key, part):
    sample = jnp.clip(jax.random.normal(jax.random.fold_in(key, 2), (NFT, NST, TILE, H * HD)), -4.0, 4.0)
    return sample.astype(jnp.bfloat16)


def draw_offsets(key, part):
    flips = jax.random.randint(jax.random.fold_in(key, 7), (H // 2,), 0, 2)
    second_kind = jnp.stack([flips, 1 - flips], axis=1).reshape(H)
    outer_steps = jnp.repeat(jnp.arange(3, dtype=jnp.int32) - 1, 3)
    inner_steps = jnp.tile(jnp.arange(3, dtype=jnp.int32) - 1, 3)
    zeros_nine = jnp.zeros((9,), jnp.int32)
    spatial = jnp.stack([zeros_nine, outer_steps, inner_steps], axis=1)
    temporal = jnp.stack([outer_steps, inner_steps, zeros_nine], axis=1)
    table = jnp.where(second_kind[:, None, None] == 1, temporal[None], spatial[None])
    head_keys = jax.random.split(jax.random.fold_in(key, 8), H)
    orders = jax.vmap(lambda head_key: jax.random.permutation(head_key, 9))(head_keys).astype(jnp.int32)
    table = jnp.take_along_axis(table, orders[:, :, None], axis=1)
    return table.astype(jnp.int32)


def draw_counts(key, part):
    levels = jax.random.randint(jax.random.fold_in(key, 5), (NFT, NST), 1, TF * TH + 1)
    frame_ids = jnp.arange(NFT)[:, None]
    spot_ids = jnp.arange(NST)[None, :]
    row_ids = spot_ids // NCT
    border = (frame_ids == NFT - 1) | (row_ids == NST // NCT - 1)
    units = jnp.where(border, levels, TF * TH)
    units = jnp.where((frame_ids == NFT - 1) & (spot_ids == NST - 1), 1, units)
    return (units * TW).astype(jnp.int32)


def block_levels(stream_key, dims, pieces, least, top_value):
    loudness = 1.0
    for position, shards_of in pieces:
        draws = jax.random.uniform(jax.random.fold_in(jax.random.fold_in(stream_key, 6), position), (shards_of,), jnp.float32, least / len(pieces), top_value / len(pieces))
        loudness = loudness * jnp.repeat(jnp.exp(draws), dims[position] // shards_of).reshape((-1,) + (1,) * (len(dims) - 1 - position))
    return loudness


def noise(own_key, shape, scale, bound, cuts=(), held_as=jnp.bfloat16):
    loudness = block_levels(own_key, shape, cuts, -0.22, 0.18) if cuts else 1.0
    entries = jax.random.normal(own_key, shape, jnp.float32) * scale * loudness
    return jnp.minimum(jnp.maximum(entries, -bound), bound).astype(held_as)


def setup_inputs(seed: int = 0) -> dict:
    key_list = jax.random.split(jax.random.key(seed), 7)
    queries = draw_queries(jax.random.fold_in(key_list[6], 71), 0)
    key_rows = draw_key_rows(jax.random.fold_in(key_list[6], 71), 0)
    value_rows = noise(key_list[2], (NFT, NST, TILE, D), 1.0, 6.0, ((0, 8), (1, 16), (3, 2)))
    grad_rows = noise(key_list[3], (NFT, NST, TILE, D), 1.0, 6.0, ((0, 8), (1, 16), (2, 2)))
    offsets = draw_offsets(jax.random.fold_in(key_list[6], 71), 0)
    counts = draw_counts(jax.random.fold_in(key_list[6], 71), 0)
    return dict(queries=queries, key_rows=key_rows, value_rows=value_rows, grad_rows=grad_rows, offsets=offsets, counts=counts)


def reference(queries, key_rows, value_rows, grad_rows, offsets, counts):
    frame_count, spot_count, tile_len, model_width = queries.shape
    col_count = NCT
    row_count = spot_count // col_count
    head_count = offsets.shape[0]
    window = offsets.shape[1]
    head_dim = model_width // head_count
    score_scale = 1.0 / math.sqrt(head_dim)
    key_split = key_rows.reshape(frame_count, spot_count, tile_len, head_count, head_dim)
    value_split = value_rows.reshape(frame_count, spot_count, tile_len, head_count, head_dim)
    positions = jnp.arange(tile_len, dtype=jnp.int32)
    live_rows = positions[None, None, :] < counts[:, :, None]
    masked = jnp.where(live_rows[..., None], grad_rows, jnp.zeros_like(grad_rows))
    head_ids = jnp.broadcast_to(jnp.arange(head_count, dtype=jnp.int32)[:, None], (head_count, window))
    anchor = jnp.zeros((), jnp.int32)

    def one_tile(tile_at, state):
        query_out, key_total, value_total = state
        tile_at = jnp.asarray(tile_at).astype(jnp.int32)
        frame_at = (tile_at // spot_count).astype(jnp.int32)
        spot_at = (tile_at % spot_count).astype(jnp.int32)
        row_at = spot_at // col_count
        col_at = spot_at % col_count
        near_frame = frame_at + offsets[:, :, 0]
        near_row = row_at + offsets[:, :, 1]
        near_col = col_at + offsets[:, :, 2]
        inside = (near_frame >= 0) & (near_frame < frame_count) & (near_row >= 0) & (near_row < row_count) & (near_col >= 0) & (near_col < col_count)
        frame_pick = jnp.clip(near_frame, 0, frame_count - 1).astype(jnp.int32)
        spot_pick = (jnp.clip(near_row, 0, row_count - 1) * col_count + jnp.clip(near_col, 0, col_count - 1)).astype(jnp.int32)
        live_count = jnp.where(inside, counts[frame_pick, spot_pick], 0)
        live_keys = positions[None, None, :] < live_count[:, :, None]
        key_window = key_split[frame_pick, spot_pick, :, head_ids, :].astype(jnp.float32)
        value_window = value_split[frame_pick, spot_pick, :, head_ids, :].astype(jnp.float32)
        query_tile = queries[frame_at, spot_at].reshape(tile_len, head_count, head_dim).astype(jnp.float32)
        grad_tile = masked[frame_at, spot_at].reshape(tile_len, head_count, head_dim).astype(jnp.float32)
        scores = jnp.einsum('ihe,houe->hiou', query_tile, key_window) * score_scale
        scores = jnp.where(live_keys[:, None], scores, -jnp.inf)
        row_max = lax.optimization_barrier(jnp.max(scores, axis=(2, 3), keepdims=True))
        log_total = row_max + jnp.log(lax.optimization_barrier(jnp.sum(jnp.exp(scores - row_max), axis=(2, 3), keepdims=True)))
        softmax = jnp.exp(scores - log_total)
        grad_softmax = jnp.einsum('ihe,houe->hiou', grad_tile, value_window)
        row_dot = lax.optimization_barrier(jnp.sum(softmax * grad_softmax, axis=(2, 3), keepdims=True))
        grad_scores = (softmax * (grad_softmax - row_dot)).astype(jnp.bfloat16)
        softmax_low = softmax.astype(jnp.bfloat16)
        grad_scores = lax.optimization_barrier(grad_scores).astype(jnp.float32)
        softmax_low = lax.optimization_barrier(softmax_low).astype(jnp.float32)
        query_grad = jnp.einsum('hiou,houe->ihe', grad_scores, key_window) * score_scale
        query_grad = query_grad.reshape(1, 1, tile_len, model_width).astype(jnp.bfloat16)
        query_out = lax.dynamic_update_slice(query_out, query_grad, (frame_at, spot_at, anchor, anchor))
        value_part = jnp.einsum('hiou,ihe->houe', softmax_low, grad_tile)
        key_part = jnp.einsum('hiou,ihe->houe', grad_scores, query_tile) * score_scale
        key_total = key_total.at[frame_pick, spot_pick, :, head_ids, :].add(key_part)
        value_total = value_total.at[frame_pick, spot_pick, :, head_ids, :].add(value_part)
        return (query_out, key_total, value_total)
    start = (jnp.zeros_like(queries), jnp.zeros((frame_count, spot_count, tile_len, head_count, head_dim), jnp.float32), jnp.zeros((frame_count, spot_count, tile_len, head_count, head_dim), jnp.float32))
    query_out, key_total, value_total = lax.fori_loop(0, frame_count * spot_count, one_tile, start)
    grad_key = key_total.reshape(frame_count, spot_count, tile_len, model_width).astype(jnp.bfloat16)
    grad_value = value_total.reshape(frame_count, spot_count, tile_len, model_width).astype(jnp.bfloat16)
    return (query_out, grad_key, grad_value)
```

```python
import functools
import math

import jax
import jax.numpy as jnp
from jax import lax
from jax.experimental import pallas as pl
from jax.experimental.pallas import tpu as pltpu
from jax.sharding import PartitionSpec as P

NCT = 4
MESH = pl.DeviceIdType.MESH
LOG2E = 1.4426950408889634


def dot_nt(a, b):
    return lax.dot_general(a, b, (((1,), (1,)), ((), ())), preferred_element_type=jnp.float32)


def dot_nn(a, b):
    return lax.dot_general(a, b, (((1,), (0,)), ((), ())), preferred_element_type=jnp.float32)


def dot_tn(a, b):
    return lax.dot_general(a, b, (((0,), (0,)), ((), ())), preferred_element_type=jnp.float32)


def step_of(code):
    return (code * (3 * code - 5)) // 2


def kernel(
    frames,
    rows,
    cols,
    offs_ref,
    counts_ref,
    q_ref,
    k_ref,
    v_ref,
    g_ref,
    dq_ref,
    dk_ref,
    dv_ref,
    held,
    stats,
    s_scr,
    p_scr,
    gbuf,
    m_row,
    l_row,
    d_row,
    qacc,
    kacc,
    vacc,
    qres,
    kres,
    vres,
    send_sem,
    recv_sem,
    stat_send,
    stat_recv,
    g_send,
    g_recv,
):
    tile_len, width = q_ref.shape
    pairs = held.shape[1]
    hd = held.shape[4] // 2
    half = g_ref.shape[0]
    scale = 1.0 / math.sqrt(hd)
    c2 = scale * LOG2E
    frame = lax.axis_index("frame")
    tile = lax.axis_index("tile")
    section = lax.axis_index("section")
    row = tile // cols
    col = tile % cols

    def inner_pos(kind):
        return col + kind * (row - col), cols + kind * (rows - cols)

    def outer_pos(kind):
        return row + kind * (frame - row), rows + kind * (frames - rows)

    def has_inner(kind, step):
        pos, size = inner_pos(kind)
        return (pos + step >= 0) & (pos + step < size)

    def has_outer(kind, step):
        pos, size = outer_pos(kind)
        return (pos + step >= 0) & (pos + step < size)

    def inner_id(kind, step):
        return {"tile": tile + step * (1 + kind * (cols - 1))}

    def outer_id(kind, step):
        return {"tile": tile + step * (1 - kind) * cols, "frame": frame + step * kind}

    def big(kind, pair, part, src, dst, device):
        return pltpu.make_async_remote_copy(
            src_ref=held.at[kind, pair, part, src],
            dst_ref=held.at[kind, pair, part, dst],
            send_sem=send_sem.at[kind, pair, part, dst],
            recv_sem=recv_sem.at[kind, pair, part, dst],
            device_id=device,
            device_id_type=MESH,
        )

    def small(kind, pair, part, src, dst, device):
        return pltpu.make_async_remote_copy(
            src_ref=stats.at[kind, pair, src],
            dst_ref=stats.at[kind, pair, dst],
            send_sem=stat_send.at[kind, pair, dst],
            recv_sem=stat_recv.at[kind, pair, dst],
            device_id=device,
            device_id_type=MESH,
        )

    def own(copy, kind, pair, part):
        for code, step in ((1, 1), (2, -1)):

            @pl.when(has_inner(kind, step))
            def _():
                copy(kind, pair, part, 0, code, inner_id(kind, step)).start()

            @pl.when(has_outer(kind, step))
            def _():
                copy(kind, pair, part, 0, 3 * code, outer_id(kind, step)).start()

    def pump(copy, kind, pair, part):
        for j, from_step in ((1, -1), (2, 1)):

            @pl.when(has_inner(kind, from_step))
            def _():
                copy(kind, pair, part, 0, j, inner_id(kind, from_step)).wait_recv()
                for code, step in ((1, 1), (2, -1)):

                    @pl.when(has_outer(kind, step))
                    def _():
                        copy(kind, pair, part, j, 3 * code + j, outer_id(kind, step)).start()

    def drain(copy, kind, pair, part):
        for code, step in ((1, 1), (2, -1)):

            @pl.when(has_inner(kind, step))
            def _():
                copy(kind, pair, part, 0, code, inner_id(kind, step)).wait_send()

            @pl.when(has_outer(kind, step))
            def _():
                copy(kind, pair, part, 0, 3 * code, outer_id(kind, step)).wait_send()
                for j, from_step in ((1, -1), (2, 1)):

                    @pl.when(has_inner(kind, from_step))
                    def _():
                        copy(kind, pair, part, j, 3 * code + j, outer_id(kind, step)).wait_send()

    def own_chunk(chunk):
        for kind in (0, 1):
            own(big, kind, lax.rem(chunk, pairs), chunk // pairs)

    def pump_chunk(chunk):
        for kind in (0, 1):
            pump(big, kind, lax.rem(chunk, pairs), chunk // pairs)

    flags = []
    for pair in range(pairs):
        seen = jnp.int32(0)
        for o in range(offs_ref.shape[1]):
            step = offs_ref[2 * pair, o, 0]
            seen = seen + step * step
        flags.append(seen > 0)

    def head(ref, h):
        return ref[:, h * hd : (h + 1) * hd]

    for pair in range(pairs):
        for at, ref in ((0, k_ref), (1, v_ref)):
            even, odd = head(ref, 2 * pair), head(ref, 2 * pair + 1)
            lanes = slice(at * hd, (at + 1) * hd)
            held[0, pair, 0, 0, :, lanes] = jnp.where(flags[pair], odd, even)
            held[1, pair, 0, 0, :, lanes] = jnp.where(flags[pair], even, odd)

    barrier = pltpu.get_barrier_semaphore()
    partner = {"section": 1 - section}
    pl.semaphore_signal(barrier, inc=1, device_id=partner, device_id_type=MESH)
    expected = jnp.int32(1)
    for make, has in (
        (functools.partial(inner_id, 0), functools.partial(has_inner, 0)),
        (functools.partial(outer_id, 0), functools.partial(has_outer, 0)),
        (functools.partial(outer_id, 1), functools.partial(has_outer, 1)),
    ):
        for step in (1, -1):
            expected = expected + has(step).astype(jnp.int32)

            @pl.when(has(step))
            def _():
                pl.semaphore_signal(barrier, inc=1, device_id=make(step), device_id_type=MESH)

    pl.semaphore_wait(barrier, expected)

    swap = pltpu.make_async_remote_copy(
        src_ref=g_ref.at[:, pl.ds(pl.multiple_of((1 - section) * width, 128), width)],
        dst_ref=gbuf.at[pl.ds(pl.multiple_of(section * half, 16), half)],
        send_sem=g_send,
        recv_sem=g_recv,
        device_id=partner,
        device_id_type=MESH,
    )
    swap.start()
    for chunk in range(pairs):
        own_chunk(chunk)

    gbuf[pl.ds(pl.multiple_of(section * half, 16), half), :] = g_ref[
        :, pl.ds(pl.multiple_of(section * width, 128), width)
    ]
    swap.wait()
    own_count = counts_ref[frame, tile]
    live = lax.broadcasted_iota(jnp.int32, (tile_len, hd), 0) < own_count
    for pair in range(pairs):
        even, odd = head(q_ref, 2 * pair), head(q_ref, 2 * pair + 1)
        held[0, pair, 1, 0, :, 0:hd] = jnp.where(flags[pair], odd, even)
        held[1, pair, 1, 0, :, 0:hd] = jnp.where(flags[pair], even, odd)
        even = jnp.where(live, head(gbuf, 2 * pair).astype(jnp.float32), 0.0).astype(jnp.bfloat16)
        odd = jnp.where(live, head(gbuf, 2 * pair + 1).astype(jnp.float32), 0.0).astype(jnp.bfloat16)
        held[0, pair, 1, 0, :, hd:] = jnp.where(flags[pair], odd, even)
        held[1, pair, 1, 0, :, hd:] = jnp.where(flags[pair], even, odd)

    pump_chunk(0)
    pump_chunk(1)

    def groups(x):
        return x.reshape(x.shape[0] // 8, 8, x.shape[1])

    def slot_steps(slot):
        return step_of(slot // 3), step_of(lax.rem(slot, 3))

    def present(kind, slot):
        outer, inner = slot_steps(slot)
        return has_outer(kind, outer) & has_inner(kind, inner)

    def query_pass(kind, pair):
        query = held[kind, pair, 1, 0, :, 0:hd]
        grad = held[kind, pair, 1, 0, :, hd:]
        m_row[...] = jnp.full(m_row.shape, -1e30, jnp.float32)
        l_row[...] = jnp.zeros_like(l_row)
        d_row[...] = jnp.zeros_like(d_row)
        qacc[...] = jnp.zeros_like(qacc)

        @pl.loop(0, 9)
        def _(slot):
            @pl.when(present(kind, slot))
            def _():
                outer, inner = slot_steps(slot)

                @pl.when(slot >= 3)
                def _():
                    big(kind, pair, 0, 0, slot, outer_id(kind, outer)).wait_recv()

                s_scr[slot] = dot_nt(held[kind, pair, 0, slot, :, 0:hd], query)
                p_scr[slot] = dot_nt(held[kind, pair, 0, slot, :, hd:], grad)
                frame_at = frame + kind * outer
                row_at = row + kind * inner + (1 - kind) * outer
                col_at = col + (1 - kind) * inner

                @pl.when((frame_at == frames - 1) | (row_at == rows - 1))
                def _():
                    count = counts_ref[frame_at, row_at * cols + col_at]
                    inside = lax.broadcasted_iota(jnp.int32, (tile_len, tile_len), 0) < count
                    s_scr[slot] = jnp.where(inside, s_scr[slot], -1e30)

                m_row[...] = jnp.maximum(m_row[...], jnp.max(groups(s_scr[slot]), axis=0))

        top = jnp.max(m_row[...], axis=0, keepdims=True) * c2

        @pl.loop(0, 9)
        def _(slot):
            @pl.when(present(kind, slot))
            def _():
                e = jnp.exp2(s_scr[slot] * c2 - top)
                s_scr[slot] = e
                l_row[...] += jnp.sum(groups(e), axis=0)
                d_row[...] += jnp.sum(groups(e * p_scr[slot]), axis=0)

        total = jnp.sum(l_row[...], axis=0, keepdims=True)
        inv = 1.0 / total
        dot_row = jnp.sum(d_row[...], axis=0, keepdims=True) * inv
        stats[kind, pair, 0, 0:1, :] = top + jnp.log(total) * LOG2E
        stats[kind, pair, 0, 1:2, :] = dot_row

        @pl.loop(0, 9)
        def _(slot):
            @pl.when(present(kind, slot))
            def _():
                ds = (s_scr[slot] * inv * (p_scr[slot] - dot_row)).astype(jnp.bfloat16)
                qacc[...] += dot_tn(held[kind, pair, 0, slot, :, 0:hd], ds)

        qres[kind, pair] = (qacc[...].T * scale).astype(jnp.bfloat16)
        own(small, kind, pair, 0)

    def key_pass(kind, pair):
        keys = held[kind, pair, 0, 0, :, 0:hd]
        values = held[kind, pair, 0, 0, :, hd:]
        kacc[...] = jnp.zeros_like(kacc)
        vacc[...] = jnp.zeros_like(vacc)

        @pl.loop(0, 9)
        def _(slot):
            @pl.when(present(kind, slot))
            def _():
                outer, _ = slot_steps(slot)

                @pl.when(slot >= 3)
                def _():
                    big(kind, pair, 1, 0, slot, outer_id(kind, outer)).wait_recv()
                    small(kind, pair, 0, 0, slot, outer_id(kind, outer)).wait_recv()

                query = held[kind, pair, 1, slot, :, 0:hd]
                grad = held[kind, pair, 1, slot, :, hd:]
                soft = jnp.exp2(dot_nt(keys, query) * c2 - stats[kind, pair, slot, 0:1, :])
                vacc[...] += dot_nn(soft.astype(jnp.bfloat16), grad)
                ds = soft * (dot_nt(values, grad) - stats[kind, pair, slot, 1:2, :])
                kacc[...] += dot_nn(ds.astype(jnp.bfloat16), query)

        kres[kind, pair] = jnp.where(live, kacc[...] * scale, 0.0).astype(jnp.bfloat16)
        vres[kind, pair] = jnp.where(live, vacc[...], 0.0).astype(jnp.bfloat16)

    @pl.loop(0, pairs)
    def _(pair):
        own_chunk(pair + pairs)
        pump_chunk(pair + 2)

        @pl.when(pair >= 1)
        def _():
            for kind in (0, 1):
                pump(small, kind, pair - 1, 0)

        @pl.loop(0, 2)
        def _(kind):
            query_pass(kind, pair)

    pump_chunk(jnp.int32(2 * pairs - 1))
    for kind in (0, 1):
        pump(small, kind, pairs - 1, 0)

    @pl.loop(0, pairs)
    def _(pair):
        @pl.loop(0, 2)
        def _(kind):
            key_pass(kind, pair)

    for pair in range(pairs):
        for res, out in ((qres, dq_ref), (kres, dk_ref), (vres, dv_ref)):
            plane, across = res[0, pair], res[1, pair]
            at = 2 * pair * hd
            out[:, at : at + hd] = jnp.where(flags[pair], across, plane)
            out[:, at + hd : at + 2 * hd] = jnp.where(flags[pair], plane, across)

    @pl.loop(0, pairs)
    def _(pair):
        @pl.loop(0, 2)
        def _(kind):
            drain(big, kind, pair, 0)
            drain(big, kind, pair, 1)
            drain(small, kind, pair, 0)


def solution(mesh):
    frames = mesh.shape["frame"]
    cols = NCT
    rows = mesh.shape["tile"] // cols

    def local(queries, key_rows, value_rows, grad_rows, offsets, counts):
        tile_len, width = queries.shape[2:]
        heads = offsets.shape[0]
        pairs = heads // 2
        hd = width // heads
        vmem = pl.BlockSpec(memory_space=pltpu.VMEM)
        smem = pl.BlockSpec(memory_space=pltpu.SMEM)
        out = jax.ShapeDtypeStruct((tile_len, width), jnp.bfloat16)
        f32 = jnp.float32
        low = jnp.bfloat16
        dq, dk, dv = pl.pallas_call(
            functools.partial(kernel, frames, rows, cols),
            out_shape=(out, out, out),
            in_specs=[smem, smem, vmem, vmem, vmem, vmem],
            out_specs=(vmem, vmem, vmem),
            scratch_shapes=[
                pltpu.VMEM((2, pairs, 2, 9, tile_len, 2 * hd), low),
                pltpu.VMEM((2, pairs, 9, 8, tile_len), f32),
                pltpu.VMEM((9, tile_len, tile_len), f32),
                pltpu.VMEM((9, tile_len, tile_len), f32),
                pltpu.VMEM((tile_len, width), low),
                pltpu.VMEM((8, tile_len), f32),
                pltpu.VMEM((8, tile_len), f32),
                pltpu.VMEM((8, tile_len), f32),
                pltpu.VMEM((hd, tile_len), f32),
                pltpu.VMEM((tile_len, hd), f32),
                pltpu.VMEM((tile_len, hd), f32),
                pltpu.VMEM((2, pairs, tile_len, hd), low),
                pltpu.VMEM((2, pairs, tile_len, hd), low),
                pltpu.VMEM((2, pairs, tile_len, hd), low),
                pltpu.SemaphoreType.DMA((2, pairs, 2, 9)),
                pltpu.SemaphoreType.DMA((2, pairs, 2, 9)),
                pltpu.SemaphoreType.DMA((2, pairs, 9)),
                pltpu.SemaphoreType.DMA((2, pairs, 9)),
                pltpu.SemaphoreType.DMA,
                pltpu.SemaphoreType.DMA,
            ],
            compiler_params=pltpu.CompilerParams(
                collective_id=0, has_side_effects=True, vmem_limit_bytes=48 * 1024 * 1024
            ),
        )(
            offsets,
            counts,
            queries[0, 0],
            key_rows[0, 0],
            value_rows[0, 0],
            grad_rows[0, 0],
        )
        return dq[None, None], dk[None, None], dv[None, None]

    return jax.shard_map(
        local,
        mesh=mesh,
        in_specs=(
            P("frame", "tile", None, "section"),
            P("frame", "tile", None, "section"),
            P("frame", "tile", None, "section"),
            P("frame", "tile", "section", None),
            P("section", None, None),
            P(),
        ),
        out_specs=(
            P("frame", "tile", None, "section"),
            P("frame", "tile", None, "section"),
            P("frame", "tile", None, "section"),
        ),
        check_vma=False,
    )
```

```python
import functools
import math

import jax
import jax.numpy as jnp
from jax import lax
from jax.experimental import pallas as pl
from jax.experimental.pallas import tpu as pltpu
from jax.sharding import PartitionSpec as P

NCT = 4
MESH = pl.DeviceIdType.MESH
LOG2E = 1.4426950408889634
RELAY = 2


def dot_nt(a, b):
    return lax.dot_general(a, b, (((1,), (1,)), ((), ())), preferred_element_type=jnp.float32)


def dot_nn(a, b):
    return lax.dot_general(a, b, (((1,), (0,)), ((), ())), preferred_element_type=jnp.float32)


def dot_tn(a, b):
    return lax.dot_general(a, b, (((0,), (0,)), ((), ())), preferred_element_type=jnp.float32)


def spans_frames(offs_ref, pair):
    seen = jnp.int32(0)
    for o in range(offs_ref.shape[2]):
        step = offs_ref[2 * pair, 0, o]
        seen = seen + step * step
    return seen > 0


def step_of(code):
    return (code * (3 * code - 5)) // 2


def kernel(
    frames,
    rows,
    cols,
    offs_hbm,
    counts_hbm,
    q_hbm,
    k_hbm,
    v_hbm,
    g_hbm,
    qres,
    kres,
    vres,
    offs_ref,
    counts_ref,
    q_ref,
    k_ref,
    v_ref,
    g_ref,
    held,
    stats,
    s_scr,
    p_scr,
    gbuf,
    m_row,
    l_row,
    d_row,
    qacc,
    kacc,
    vacc,
    send_sem,
    recv_sem,
    stat_send,
    stat_recv,
    g_send,
    g_recv,
    in_sem,
):
    loads = [
        pltpu.make_async_copy(src, dst, in_sem.at[at])
        for at, (src, dst) in enumerate(
            (
                (offs_hbm, offs_ref),
                (k_hbm, k_ref),
                (v_hbm, v_ref),
                (g_hbm, g_ref),
                (q_hbm, q_ref),
                (counts_hbm, counts_ref),
            )
        )
    ]
    for load in loads:
        load.start()
    tile_len, width = q_ref.shape
    pairs = held.shape[1]
    hd = held.shape[4] // 2
    half = g_ref.shape[0]
    scale = 1.0 / math.sqrt(hd)
    c2 = scale * LOG2E
    frame = lax.axis_index("frame")
    tile = lax.axis_index("tile")
    section = lax.axis_index("section")
    row = tile // cols
    col = tile % cols

    def inner_pos(kind):
        return col + kind * (row - col), cols + kind * (rows - cols)

    def outer_pos(kind):
        return row + kind * (frame - row), rows + kind * (frames - rows)

    def has_inner(kind, step):
        pos, size = inner_pos(kind)
        return (pos + step >= 0) & (pos + step < size)

    def has_outer(kind, step):
        pos, size = outer_pos(kind)
        return (pos + step >= 0) & (pos + step < size)

    def inner_id(kind, step):
        return {"tile": tile + step * (1 + kind * (cols - 1))}

    def outer_id(kind, step):
        return {"tile": tile + step * (1 - kind) * cols, "frame": frame + step * kind}

    def big(kind, pair, part, src, dst, device, at=None):
        return pltpu.make_async_remote_copy(
            src_ref=held.at[kind, pair, part, src],
            dst_ref=held.at[kind, pair, part, dst],
            send_sem=send_sem.at[kind, pair, part, dst if at is None else at],
            recv_sem=recv_sem.at[kind, pair, part, dst],
            device_id=device,
            device_id_type=MESH,
        )

    def small(kind, pair, part, src, dst, device, at=None):
        return pltpu.make_async_remote_copy(
            src_ref=stats.at[kind, pair, src],
            dst_ref=stats.at[kind, pair, dst],
            send_sem=stat_send.at[kind, pair, dst],
            recv_sem=stat_recv.at[kind, pair, dst],
            device_id=device,
            device_id_type=MESH,
        )

    mid = frames // 2 - 1
    via_up = frames - 1 if RELAY == 1 else 0
    via_down = frames - 1 - via_up

    def outer_copy(copy, kind, pair, part, code, step, j):
        dst = 3 * code + j
        device = outer_id(kind, step)
        if RELAY and copy is big and kind == 1 and j:
            aside = (part * pairs + pair < 2 * pairs - j).astype(jnp.int32)
            if step == 1:
                crossing = (frame == mid).astype(jnp.int32) * aside
                device["frame"] = frame + 1 + crossing * (via_up - mid - 1)
                land = dst + crossing * (3 if via_up else 0)
            else:
                crossing = (frame == mid + 1).astype(jnp.int32) * aside
                device["frame"] = frame - 1 + crossing * (via_down - mid)
                land = dst - crossing * (0 if via_down else 3)
            return copy(kind, pair, part, j, land, device, dst)
        return copy(kind, pair, part, j, dst, device)

    def relay_copy(pair, part, j, first):
        up = (via_up == 0) == first
        src = (3 if first else 6) + j
        return big(1, pair, part, src, (3 if up else 6) + j, {"frame": mid + 1 if up else mid}, (6 if first else 3) + j)

    def for_relays(pair, part, act):
        if not RELAY:
            return
        for first in (True, False):
            for j, from_step in ((1, -1), (2, 1)):
                go = has_inner(1, from_step) & (frame == (0 if first else frames - 1))
                go = go & (part * pairs + pair < 2 * pairs - j)

                @pl.when(go)
                def _():
                    act(relay_copy(pair, part, j, first), pair, part, (3 if first else 6) + j)

    def forward(copy, pair, part, slot):
        big(1, pair, part, 0, slot, {"frame": mid}).wait_recv()
        copy.start()

    def relay_chunk(chunk):
        for_relays(lax.rem(chunk, pairs), chunk // pairs, forward)

    def own(copy, kind, pair, part):
        for code, step in ((1, 1), (2, -1)):

            @pl.when(has_inner(kind, step))
            def _():
                copy(kind, pair, part, 0, code, inner_id(kind, step)).start()

            @pl.when(has_outer(kind, step))
            def _():
                outer_copy(copy, kind, pair, part, code, step, 0).start()

    def pump(copy, kind, pair, part):
        for j, from_step in ((1, -1), (2, 1)):

            @pl.when(has_inner(kind, from_step))
            def _():
                copy(kind, pair, part, 0, j, inner_id(kind, from_step)).wait_recv()
                for code, step in ((1, 1), (2, -1)):

                    @pl.when(has_outer(kind, step))
                    def _():
                        outer_copy(copy, kind, pair, part, code, step, j).start()

    def drain(copy, kind, pair, part):
        for code, step in ((1, 1), (2, -1)):

            @pl.when(has_inner(kind, step))
            def _():
                copy(kind, pair, part, 0, code, inner_id(kind, step)).wait_send()

            @pl.when(has_outer(kind, step))
            def _():
                outer_copy(copy, kind, pair, part, code, step, 0).wait_send()
                for j, from_step in ((1, -1), (2, 1)):

                    @pl.when(has_inner(kind, from_step))
                    def _():
                        outer_copy(copy, kind, pair, part, code, step, j).wait_send()

    def own_chunk(chunk):
        for kind in (0, 1):
            own(big, kind, lax.rem(chunk, pairs), chunk // pairs)

    def pump_chunk(kind, chunk):
        pump(big, kind, lax.rem(chunk, pairs), chunk // pairs)

    barrier = pltpu.get_barrier_semaphore()
    partner = {"section": 1 - section}
    pl.semaphore_signal(barrier, inc=1, device_id=partner, device_id_type=MESH)
    expected = jnp.int32(1)
    for make, has in (
        (functools.partial(inner_id, 0), functools.partial(has_inner, 0)),
        (functools.partial(outer_id, 0), functools.partial(has_outer, 0)),
        (functools.partial(outer_id, 1), functools.partial(has_outer, 1)),
    ):
        for step in (1, -1):
            expected = expected + has(step).astype(jnp.int32)

            @pl.when(has(step))
            def _():
                pl.semaphore_signal(barrier, inc=1, device_id=make(step), device_id_type=MESH)

    if RELAY:
        for ends, others in (((0, frames - 1), (mid, mid + 1)), ((mid, mid + 1), (0, frames - 1))):
            inside = (frame == ends[0]) | (frame == ends[1])
            expected = expected + 2 * inside.astype(jnp.int32)

            @pl.when(inside)
            def _():
                for other in others:
                    pl.semaphore_signal(barrier, inc=1, device_id={"frame": other}, device_id_type=MESH)

    loads[0].wait()
    flags = [spans_frames(offs_ref, pair) for pair in range(pairs)]

    def head(ref, h):
        return ref[:, h * hd : (h + 1) * hd]

    def pack_keys(pair):
        for at, ref in ((0, k_ref), (1, v_ref)):
            even, odd = head(ref, 2 * pair), head(ref, 2 * pair + 1)
            lanes = slice(at * hd, (at + 1) * hd)
            held[0, pair, 0, 0, :, lanes] = jnp.where(flags[pair], odd, even)
            held[1, pair, 0, 0, :, lanes] = jnp.where(flags[pair], even, odd)

    loads[1].wait()
    loads[2].wait()
    pack_keys(0)
    loads[3].wait()
    pl.semaphore_wait(barrier, expected)

    swap = pltpu.make_async_remote_copy(
        src_ref=g_ref.at[:, pl.ds(pl.multiple_of((1 - section) * width, 128), width)],
        dst_ref=gbuf.at[pl.ds(pl.multiple_of(section * half, 16), half)],
        send_sem=g_send,
        recv_sem=g_recv,
        device_id=partner,
        device_id_type=MESH,
    )
    swap.start()
    own_chunk(0)
    for pair in range(1, pairs):
        pack_keys(pair)
    for chunk in range(1, pairs):
        own_chunk(chunk)

    for kind in (0, 1):
        for j, from_step in ((1, -1), (2, 1)):

            @pl.when(jnp.logical_not(has_inner(kind, from_step)))
            def _():
                @pl.loop(0, pairs)
                def _(pair):
                    @pl.loop(0, 3)
                    def _(g):
                        held[kind, pair, 0, 3 * g + j] = jnp.zeros(held.shape[4:], held.dtype)
                        held[kind, pair, 1, 3 * g + j] = jnp.zeros(held.shape[4:], held.dtype)
                        stats[kind, pair, 3 * g + j] = jnp.zeros(stats.shape[3:], stats.dtype)

    gbuf[pl.ds(pl.multiple_of(section * half, 16), half), :] = g_ref[
        :, pl.ds(pl.multiple_of(section * width, 128), width)
    ]
    loads[4].wait()
    loads[5].wait()
    swap.wait()
    own_count = counts_ref[frame, tile]
    live = lax.broadcasted_iota(jnp.int32, (tile_len, hd), 0) < own_count
    for pair in range(pairs):
        even, odd = head(q_ref, 2 * pair), head(q_ref, 2 * pair + 1)
        held[0, pair, 1, 0, :, 0:hd] = jnp.where(flags[pair], odd, even)
        held[1, pair, 1, 0, :, 0:hd] = jnp.where(flags[pair], even, odd)
        even = jnp.where(live, head(gbuf, 2 * pair).astype(jnp.float32), 0.0).astype(jnp.bfloat16)
        odd = jnp.where(live, head(gbuf, 2 * pair + 1).astype(jnp.float32), 0.0).astype(jnp.bfloat16)
        held[0, pair, 1, 0, :, hd:] = jnp.where(flags[pair], odd, even)
        held[1, pair, 1, 0, :, hd:] = jnp.where(flags[pair], even, odd)

    for chunk in range(pairs):
        for kind in (0, 1):
            pump_chunk(kind, chunk)
    relay_chunk(0)
    relay_chunk(1)

    crossing = (frame == mid) | (frame == mid + 1)
    first_kind = 1 - crossing.astype(jnp.int32)

    def groups(x):
        return x.reshape(x.shape[0] // 8, 8, x.shape[1])

    def stacked(kind, pair, part, g, at):
        block = held[kind, pair, part, pl.ds(3 * g, 3), :, at * hd : (at + 1) * hd]
        return block.reshape(3 * tile_len, hd)

    def await_group(copy, kind, pair, part, g):
        @pl.when(g > 0)
        def _():
            for j, from_step in ((0, 0), (1, -1), (2, 1)):

                @pl.when(has_inner(kind, from_step))
                def _():
                    copy(kind, pair, part, 0, 3 * g + j, outer_id(kind, step_of(g))).wait_recv()

    def query_group(kind, pair, g, masked):
        query = held[kind, pair, 1, 0, :, 0:hd]
        grad = held[kind, pair, 1, 0, :, hd:]
        s = dot_nt(stacked(kind, pair, 0, g, 0), query)
        if masked:
            outer = step_of(g)
            at = lax.broadcasted_iota(jnp.int32, (tile_len, tile_len), 0)
            blocks = []
            for j, inner in ((0, 0), (1, -1), (2, 1)):
                frame_at = frame + kind * outer
                row_at = jnp.clip(row + kind * inner + (1 - kind) * outer, 0, rows - 1)
                col_at = jnp.clip(col + (1 - kind) * inner, 0, cols - 1)
                count = counts_ref[frame_at, row_at * cols + col_at]
                count = jnp.where(has_inner(kind, inner), count, 0)
                blocks.append(jnp.where(at < count, s[j * tile_len : (j + 1) * tile_len], -1e30))
            s = jnp.concatenate(blocks, axis=0)
        top = jnp.max(jnp.max(groups(s), axis=0), axis=0, keepdims=True) * c2
        e = jnp.exp2(s * c2 - top)
        p = dot_nt(stacked(kind, pair, 0, g, 1), grad)
        s_scr[g] = e
        p_scr[g] = p
        m_row[g, 0:1, :] = top
        l_row[g, 0:1, :] = jnp.sum(jnp.sum(groups(e), axis=0), axis=0, keepdims=True)
        d_row[g, 0:1, :] = jnp.sum(jnp.sum(groups(e * p), axis=0), axis=0, keepdims=True)

    def query_pass(kind, pair):
        m_row[...] = jnp.full(m_row.shape, -1e30, jnp.float32)
        l_row[...] = jnp.zeros_like(l_row)
        d_row[...] = jnp.zeros_like(d_row)
        qacc[...] = jnp.zeros_like(qacc)

        @pl.loop(0, 3)
        def _(g):
            outer = step_of(g)

            @pl.when(has_outer(kind, outer))
            def _():
                await_group(big, kind, pair, 0, g)
                inner_at, inner_size = inner_pos(kind)
                frame_at = frame + kind * outer
                lowest = row + (1 - kind) * outer + kind
                partial = (frame_at == frames - 1) | (lowest >= rows - 1)
                partial = partial | (inner_at == 0) | (inner_at == inner_size - 1)

                @pl.when(partial)
                def _():
                    query_group(kind, pair, g, True)

                @pl.when(jnp.logical_not(partial))
                def _():
                    query_group(kind, pair, g, False)

        tops = [m_row[g, 0:1, :] for g in range(3)]
        top = jnp.maximum(jnp.maximum(tops[0], tops[1]), tops[2])
        parts = [jnp.exp2(t - top) for t in tops]
        total = sum(parts[g] * l_row[g, 0:1, :] for g in range(3))
        inv = 1.0 / total
        dot_row = sum(parts[g] * d_row[g, 0:1, :] for g in range(3)) * inv
        for g in range(3):
            m_row[g, 0:1, :] = parts[g] * inv
        stats[kind, pair, 0, 0:1, :] = top + jnp.log(total) * LOG2E
        stats[kind, pair, 0, 1:2, :] = dot_row

        @pl.loop(0, 3)
        def _(g):
            @pl.when(has_outer(kind, step_of(g)))
            def _():
                ds = (s_scr[g] * m_row[g, 0:1, :] * (p_scr[g] - dot_row)).astype(jnp.bfloat16)
                qacc[...] += dot_tn(stacked(kind, pair, 0, g, 0), ds)

        qres[kind, pair] = (qacc[...].T * scale).astype(jnp.bfloat16)
        own(small, kind, pair, 0)

    def key_slots(kind, pair, slots):
        keys = held[kind, pair, 0, 0, :, 0:hd]
        values = held[kind, pair, 0, 0, :, hd:]
        query = jnp.concatenate([held[kind, pair, 1, slot, :, 0:hd] for slot in slots], axis=0)
        grad = jnp.concatenate([held[kind, pair, 1, slot, :, hd:] for slot in slots], axis=0)
        log_total = jnp.concatenate([stats[kind, pair, slot, 0:1, :] for slot in slots], axis=1)
        dot_row = jnp.concatenate([stats[kind, pair, slot, 1:2, :] for slot in slots], axis=1)
        soft = jnp.exp2(dot_nt(keys, query) * c2 - log_total)
        vacc[kind, pair] += dot_nn(soft.astype(jnp.bfloat16), grad)
        ds = soft * (dot_nt(values, grad) - dot_row)
        kacc[kind, pair] += dot_nn(ds.astype(jnp.bfloat16), query)

    def key_outer(kind, pair, j):
        has = (has_outer(kind, -1), has_outer(kind, 1))
        for g in (1, 2):

            @pl.when(has[g - 1])
            def _():
                device = outer_id(kind, step_of(g))
                big(kind, pair, 1, 0, 3 * g + j, device).wait_recv()
                small(kind, pair, 0, 0, 3 * g + j, device).wait_recv()

        @pl.when(has[0] & has[1])
        def _():
            key_slots(kind, pair, (3 + j, 6 + j))

        @pl.when(jnp.logical_not(has[0] & has[1]))
        def _():
            key_slots(kind, pair, (6 + j - 3 * has[0].astype(jnp.int32),))

    @pl.loop(0, pairs)
    def _(pair):
        own_chunk(pair + pairs)

        @pl.when(pair >= 1)
        def _():
            pump_chunk(0, pair + pairs - 1)
            for kind in (0, 1):
                pump(small, kind, pair - 1, 0)

        @pl.when(pair == 2)
        def _():
            pump_chunk(1, jnp.int32(pairs))

        @pl.loop(0, 2)
        def _(at):
            query_pass(first_kind + at * (1 - 2 * first_kind), pair)

        @pl.when(pair == 0)
        def _():
            relay_chunk(jnp.int32(2))

    pump_chunk(1, jnp.int32(pairs + 1))
    pump_chunk(0, jnp.int32(2 * pairs - 1))
    relay_chunk(jnp.int32(pairs))

    order = (
        (0, 0, 0), (0, 0, 1), (0, 0, 2), (1, 0, 0), (1, 0, 1), (1, 0, 2),
        (0, 1, 0), (1, 1, 0), (0, 1, 1), (0, 1, 2),
        (0, 2, 0), (1, 2, 0),
        (1, 1, 1), (1, 1, 2),
        (0, 2, 1), (0, 2, 2), (1, 2, 1), (1, 2, 2),
    )

    @pl.loop(0, len(order))
    def _(step):
        def pick(part):
            found = jnp.int32(0)
            for at, entry in enumerate(order):
                if entry[part]:
                    found = found + entry[part] * (step == at).astype(jnp.int32)
            return found

        later, pair, j = pick(0), pick(1), pick(2)
        kind = first_kind + later * (1 - 2 * first_kind)

        @pl.when(step == 6)
        def _():
            for kind in (0, 1):
                pump(small, kind, pairs - 1, 0)

        @pl.when(step == 8)
        def _():
            pump_chunk(1, jnp.int32(2 * pairs - 1))
            relay_chunk(jnp.int32(2 * pairs - 2))

        @pl.when(j == 0)
        def _():
            kacc[kind, pair] = jnp.zeros(kacc.shape[2:], kacc.dtype)
            vacc[kind, pair] = jnp.zeros(vacc.shape[2:], vacc.dtype)
            key_slots(kind, pair, (0, 1, 2))

        @pl.when(has_inner(kind, step_of(j)))
        def _():
            key_outer(kind, pair, j)

        @pl.when(j == 2)
        def _():
            kres[kind, pair] = jnp.where(live, kacc[kind, pair] * scale, 0.0).astype(jnp.bfloat16)
            vres[kind, pair] = jnp.where(live, vacc[kind, pair], 0.0).astype(jnp.bfloat16)

    @pl.loop(0, pairs)
    def _(pair):
        for kind in (0, 1):
            drain(big, kind, pair, 0)
            drain(big, kind, pair, 1)
            drain(small, kind, pair, 0)
        for part in (0, 1):
            for_relays(pair, part, lambda copy, *_: copy.wait_send())


def place_heads(offs_ref, qres, kres, vres, dq_ref, dk_ref, dv_ref, rows, sem):
    pairs, _, hd = qres.shape[1:]
    copies = []
    for at, (res, out) in enumerate(((qres, dq_ref), (kres, dk_ref), (vres, dv_ref))):
        for pair in range(pairs):
            flag = spans_frames(offs_ref, pair)
            plane, across = res[0, pair], res[1, pair]
            rows[at, pair, :, :hd] = jnp.where(flag, across, plane)
            rows[at, pair, :, hd:] = jnp.where(flag, plane, across)
            lanes = slice(2 * pair * hd, 2 * (pair + 1) * hd)
            copies.append(pltpu.make_async_copy(rows.at[at, pair], out.at[:, lanes], sem.at[at, pair]))
            copies[-1].start()
    for copy in copies:
        copy.wait()


def solution(mesh):
    frames = mesh.shape["frame"]
    cols = NCT
    rows = mesh.shape["tile"] // cols

    def local(queries, key_rows, value_rows, grad_rows, offsets, counts):
        tile_len, width = queries.shape[2:]
        heads = offsets.shape[0]
        pairs = heads // 2
        hd = width // heads
        vmem = pl.BlockSpec(memory_space=pltpu.VMEM)
        hbm = pl.BlockSpec(memory_space=pltpu.HBM)
        smem = pl.BlockSpec(memory_space=pltpu.SMEM)
        out = jax.ShapeDtypeStruct((tile_len, width), jnp.bfloat16)
        packed = jax.ShapeDtypeStruct((2, pairs, tile_len, hd), jnp.bfloat16)
        f32 = jnp.float32
        low = jnp.bfloat16
        steps = jnp.transpose(offsets, (0, 2, 1))
        results = pl.pallas_call(
            functools.partial(kernel, frames, rows, cols),
            out_shape=(packed, packed, packed),
            in_specs=[hbm] * 6,
            out_specs=(vmem, vmem, vmem),
            scratch_shapes=[
                pltpu.SMEM(steps.shape, jnp.int32),
                pltpu.SMEM(counts.shape, jnp.int32),
                pltpu.VMEM((tile_len, width), low),
                pltpu.VMEM((tile_len, width), low),
                pltpu.VMEM((tile_len, width), low),
                pltpu.VMEM(grad_rows.shape[2:], low),
                pltpu.VMEM((2, pairs, 2, 9, tile_len, 2 * hd), low),
                pltpu.VMEM((2, pairs, 9, 8, tile_len), f32),
                pltpu.VMEM((3, 3 * tile_len, tile_len), f32),
                pltpu.VMEM((3, 3 * tile_len, tile_len), f32),
                pltpu.VMEM((tile_len, width), low),
                pltpu.VMEM((3, 8, tile_len), f32),
                pltpu.VMEM((3, 8, tile_len), f32),
                pltpu.VMEM((3, 8, tile_len), f32),
                pltpu.VMEM((hd, tile_len), f32),
                pltpu.VMEM((2, pairs, tile_len, hd), f32),
                pltpu.VMEM((2, pairs, tile_len, hd), f32),
                pltpu.SemaphoreType.DMA((2, pairs, 2, 9)),
                pltpu.SemaphoreType.DMA((2, pairs, 2, 9)),
                pltpu.SemaphoreType.DMA((2, pairs, 9)),
                pltpu.SemaphoreType.DMA((2, pairs, 9)),
                pltpu.SemaphoreType.DMA,
                pltpu.SemaphoreType.DMA,
                pltpu.SemaphoreType.DMA((6,)),
            ],
            compiler_params=pltpu.CompilerParams(
                collective_id=0, has_side_effects=True, vmem_limit_bytes=48 * 1024 * 1024
            ),
        )(
            *(
                pltpu.with_memory_space_constraint(array, pltpu.HBM)
                for array in (steps, counts, queries[0, 0], key_rows[0, 0], value_rows[0, 0], grad_rows[0, 0])
            ),
        )
        dq, dk, dv = pl.pallas_call(
            place_heads,
            out_shape=(out, out, out),
            in_specs=[smem, vmem, vmem, vmem],
            out_specs=(hbm, hbm, hbm),
            scratch_shapes=[
                pltpu.VMEM((3, pairs, tile_len, 2 * hd), low),
                pltpu.SemaphoreType.DMA((3, pairs)),
            ],
            compiler_params=pltpu.CompilerParams(vmem_limit_bytes=8 * 1024 * 1024),
        )(steps, *results)
        return dq[None, None], dk[None, None], dv[None, None]

    return jax.shard_map(
        local,
        mesh=mesh,
        in_specs=(
            P("frame", "tile", None, "section"),
            P("frame", "tile", None, "section"),
            P("frame", "tile", None, "section"),
            P("frame", "tile", "section", None),
            P("section", None, None),
            P(),
        ),
        out_specs=(
            P("frame", "tile", None, "section"),
            P("frame", "tile", None, "section"),
            P("frame", "tile", None, "section"),
        ),
        check_vma=False,
    )
```

```python
import functools
import math

import jax
import jax.numpy as jnp
from jax import lax
from jax.experimental import pallas as pl
from jax.experimental.pallas import tpu as pltpu
from jax.sharding import PartitionSpec as P

NCT = 4
MESH = pl.DeviceIdType.MESH
LOG2E = 1.4426950408889634
RELAY = 2


def dot_nt(a, b):
    return lax.dot_general(a, b, (((1,), (1,)), ((), ())), preferred_element_type=jnp.float32)


def dot_nn(a, b):
    return lax.dot_general(a, b, (((1,), (0,)), ((), ())), preferred_element_type=jnp.float32)


def dot_tn(a, b):
    return lax.dot_general(a, b, (((0,), (0,)), ((), ())), preferred_element_type=jnp.float32)


def spans_frames(offs_ref, pair):
    seen = jnp.int32(0)
    for o in range(offs_ref.shape[2]):
        step = offs_ref[2 * pair, 0, o]
        seen = seen + step * step
    return seen > 0


def step_of(code):
    return (code * (3 * code - 5)) // 2


def kernel(
    frames,
    rows,
    cols,
    offs_hbm,
    counts_hbm,
    q_hbm,
    k_hbm,
    v_hbm,
    g_hbm,
    dq_ref,
    dk_ref,
    dv_ref,
    offs_ref,
    counts_ref,
    q_ref,
    k_ref,
    v_ref,
    g_ref,
    held,
    stats,
    s_scr,
    p_scr,
    gbuf,
    m_row,
    l_row,
    d_row,
    qacc,
    kacc,
    vacc,
    qres,
    kres,
    vres,
    send_sem,
    recv_sem,
    stat_send,
    stat_recv,
    g_send,
    g_recv,
    in_sem,
):
    loads = [
        pltpu.make_async_copy(src, dst, in_sem.at[at])
        for at, (src, dst) in enumerate(
            (
                (offs_hbm, offs_ref),
                (k_hbm, k_ref),
                (v_hbm, v_ref),
                (g_hbm, g_ref),
                (q_hbm, q_ref),
                (counts_hbm, counts_ref),
            )
        )
    ]
    for load in loads:
        load.start()
    tile_len, width = q_ref.shape
    pairs = held.shape[1]
    hd = held.shape[4] // 2
    half = g_ref.shape[0]
    scale = 1.0 / math.sqrt(hd)
    c2 = scale * LOG2E
    frame = lax.axis_index("frame")
    tile = lax.axis_index("tile")
    section = lax.axis_index("section")
    row = tile // cols
    col = tile % cols

    def inner_pos(kind):
        return col + kind * (row - col), cols + kind * (rows - cols)

    def outer_pos(kind):
        return row + kind * (frame - row), rows + kind * (frames - rows)

    def has_inner(kind, step):
        pos, size = inner_pos(kind)
        return (pos + step >= 0) & (pos + step < size)

    def has_outer(kind, step):
        pos, size = outer_pos(kind)
        return (pos + step >= 0) & (pos + step < size)

    def inner_id(kind, step):
        return {"tile": tile + step * (1 + kind * (cols - 1))}

    def outer_id(kind, step):
        return {"tile": tile + step * (1 - kind) * cols, "frame": frame + step * kind}

    def big(kind, pair, part, src, dst, device, at=None):
        return pltpu.make_async_remote_copy(
            src_ref=held.at[kind, pair, part, src],
            dst_ref=held.at[kind, pair, part, dst],
            send_sem=send_sem.at[kind, pair, part, dst if at is None else at],
            recv_sem=recv_sem.at[kind, pair, part, dst],
            device_id=device,
            device_id_type=MESH,
        )

    def small(kind, pair, part, src, dst, device, at=None):
        return pltpu.make_async_remote_copy(
            src_ref=stats.at[kind, pair, src],
            dst_ref=stats.at[kind, pair, dst],
            send_sem=stat_send.at[kind, pair, dst],
            recv_sem=stat_recv.at[kind, pair, dst],
            device_id=device,
            device_id_type=MESH,
        )

    mid = frames // 2 - 1
    via_up = frames - 1 if RELAY == 1 else 0
    via_down = frames - 1 - via_up

    def outer_copy(copy, kind, pair, part, code, step, j):
        dst = 3 * code + j
        device = outer_id(kind, step)
        if RELAY and copy is big and kind == 1 and j:
            aside = (part * pairs + pair < 2 * pairs - j).astype(jnp.int32)
            if step == 1:
                crossing = (frame == mid).astype(jnp.int32) * aside
                device["frame"] = frame + 1 + crossing * (via_up - mid - 1)
                land = dst + crossing * (3 if via_up else 0)
            else:
                crossing = (frame == mid + 1).astype(jnp.int32) * aside
                device["frame"] = frame - 1 + crossing * (via_down - mid)
                land = dst - crossing * (0 if via_down else 3)
            return copy(kind, pair, part, j, land, device, dst)
        return copy(kind, pair, part, j, dst, device)

    def relay_copy(pair, part, j, first):
        up = (via_up == 0) == first
        src = (3 if first else 6) + j
        return big(1, pair, part, src, (3 if up else 6) + j, {"frame": mid + 1 if up else mid}, (6 if first else 3) + j)

    def for_relays(pair, part, act):
        if not RELAY:
            return
        for first in (True, False):
            for j, from_step in ((1, -1), (2, 1)):
                go = has_inner(1, from_step) & (frame == (0 if first else frames - 1))
                go = go & (part * pairs + pair < 2 * pairs - j)

                @pl.when(go)
                def _():
                    act(relay_copy(pair, part, j, first), pair, part, (3 if first else 6) + j)

    def forward(copy, pair, part, slot):
        big(1, pair, part, 0, slot, {"frame": mid}).wait_recv()
        copy.start()

    def relay_chunk(chunk):
        for_relays(lax.rem(chunk, pairs), chunk // pairs, forward)

    def own(copy, kind, pair, part):
        for code, step in ((1, 1), (2, -1)):

            @pl.when(has_inner(kind, step))
            def _():
                copy(kind, pair, part, 0, code, inner_id(kind, step)).start()

            @pl.when(has_outer(kind, step))
            def _():
                outer_copy(copy, kind, pair, part, code, step, 0).start()

    def pump(copy, kind, pair, part):
        for j, from_step in ((1, -1), (2, 1)):

            @pl.when(has_inner(kind, from_step))
            def _():
                copy(kind, pair, part, 0, j, inner_id(kind, from_step)).wait_recv()
                for code, step in ((1, 1), (2, -1)):

                    @pl.when(has_outer(kind, step))
                    def _():
                        outer_copy(copy, kind, pair, part, code, step, j).start()

    def drain(copy, kind, pair, part):
        for code, step in ((1, 1), (2, -1)):

            @pl.when(has_inner(kind, step))
            def _():
                copy(kind, pair, part, 0, code, inner_id(kind, step)).wait_send()

            @pl.when(has_outer(kind, step))
            def _():
                outer_copy(copy, kind, pair, part, code, step, 0).wait_send()
                for j, from_step in ((1, -1), (2, 1)):

                    @pl.when(has_inner(kind, from_step))
                    def _():
                        outer_copy(copy, kind, pair, part, code, step, j).wait_send()

    def own_chunk(chunk):
        for kind in (0, 1):
            own(big, kind, lax.rem(chunk, pairs), chunk // pairs)

    def pump_chunk(kind, chunk):
        pump(big, kind, lax.rem(chunk, pairs), chunk // pairs)

    barrier = pltpu.get_barrier_semaphore()
    partner = {"section": 1 - section}
    pl.semaphore_signal(barrier, inc=1, device_id=partner, device_id_type=MESH)
    expected = jnp.int32(1)
    for make, has in (
        (functools.partial(inner_id, 0), functools.partial(has_inner, 0)),
        (functools.partial(outer_id, 0), functools.partial(has_outer, 0)),
        (functools.partial(outer_id, 1), functools.partial(has_outer, 1)),
    ):
        for step in (1, -1):
            expected = expected + has(step).astype(jnp.int32)

            @pl.when(has(step))
            def _():
                pl.semaphore_signal(barrier, inc=1, device_id=make(step), device_id_type=MESH)

    if RELAY:
        for ends, others in (((0, frames - 1), (mid, mid + 1)), ((mid, mid + 1), (0, frames - 1))):
            inside = (frame == ends[0]) | (frame == ends[1])
            expected = expected + 2 * inside.astype(jnp.int32)

            @pl.when(inside)
            def _():
                for other in others:
                    pl.semaphore_signal(barrier, inc=1, device_id={"frame": other}, device_id_type=MESH)

    loads[0].wait()
    flags = [spans_frames(offs_ref, pair) for pair in range(pairs)]

    def head(ref, h):
        return ref[:, h * hd : (h + 1) * hd]

    def pack_keys(pair):
        for at, ref in ((0, k_ref), (1, v_ref)):
            even, odd = head(ref, 2 * pair), head(ref, 2 * pair + 1)
            lanes = slice(at * hd, (at + 1) * hd)
            held[0, pair, 0, 0, :, lanes] = jnp.where(flags[pair], odd, even)
            held[1, pair, 0, 0, :, lanes] = jnp.where(flags[pair], even, odd)

    loads[1].wait()
    loads[2].wait()
    pack_keys(0)
    loads[3].wait()
    pl.semaphore_wait(barrier, expected)

    swap = pltpu.make_async_remote_copy(
        src_ref=g_ref.at[:, pl.ds(pl.multiple_of((1 - section) * width, 128), width)],
        dst_ref=gbuf.at[pl.ds(pl.multiple_of(section * half, 16), half)],
        send_sem=g_send,
        recv_sem=g_recv,
        device_id=partner,
        device_id_type=MESH,
    )
    swap.start()
    own_chunk(0)
    for pair in range(1, pairs):
        pack_keys(pair)
    for chunk in range(1, pairs):
        own_chunk(chunk)

    for kind in (0, 1):
        for j, from_step in ((1, -1), (2, 1)):

            @pl.when(jnp.logical_not(has_inner(kind, from_step)))
            def _():
                @pl.loop(0, pairs)
                def _(pair):
                    @pl.loop(0, 3)
                    def _(g):
                        held[kind, pair, 0, 3 * g + j] = jnp.zeros(held.shape[4:], held.dtype)
                        held[kind, pair, 1, 3 * g + j] = jnp.zeros(held.shape[4:], held.dtype)
                        stats[kind, pair, 3 * g + j] = jnp.zeros(stats.shape[3:], stats.dtype)

    gbuf[pl.ds(pl.multiple_of(section * half, 16), half), :] = g_ref[
        :, pl.ds(pl.multiple_of(section * width, 128), width)
    ]
    loads[4].wait()
    loads[5].wait()
    swap.wait()
    own_count = counts_ref[frame, tile]
    live = lax.broadcasted_iota(jnp.int32, (tile_len, hd), 0) < own_count
    for pair in range(pairs):
        even, odd = head(q_ref, 2 * pair), head(q_ref, 2 * pair + 1)
        held[0, pair, 1, 0, :, 0:hd] = jnp.where(flags[pair], odd, even)
        held[1, pair, 1, 0, :, 0:hd] = jnp.where(flags[pair], even, odd)
        even = jnp.where(live, head(gbuf, 2 * pair).astype(jnp.float32), 0.0).astype(jnp.bfloat16)
        odd = jnp.where(live, head(gbuf, 2 * pair + 1).astype(jnp.float32), 0.0).astype(jnp.bfloat16)
        held[0, pair, 1, 0, :, hd:] = jnp.where(flags[pair], odd, even)
        held[1, pair, 1, 0, :, hd:] = jnp.where(flags[pair], even, odd)

    for chunk in range(pairs):
        for kind in (0, 1):
            pump_chunk(kind, chunk)
    relay_chunk(0)
    relay_chunk(1)

    crossing = (frame == mid) | (frame == mid + 1)
    first_kind = 1 - crossing.astype(jnp.int32)

    def groups(x):
        return x.reshape(x.shape[0] // 8, 8, x.shape[1])

    def await_group(copy, kind, pair, part, g):
        @pl.when(g > 0)
        def _():
            for j, from_step in ((0, 0), (1, -1), (2, 1)):

                @pl.when(has_inner(kind, from_step))
                def _():
                    copy(kind, pair, part, 0, 3 * g + j, outer_id(kind, step_of(g))).wait_recv()

    def query_group(kind, pair, g, masked):
        query = held[kind, pair, 1, 0, :, 0:hd]
        grad = held[kind, pair, 1, 0, :, hd:]
        outer = step_of(g)

        def products(slot):
            return dot_nt(held[kind, pair, 0, slot, :, 0:hd], query), dot_nt(held[kind, pair, 0, slot, :, hd:], grad)

        ahead = products(3 * g)
        for j, inner in ((0, 0), (1, -1), (2, 1)):
            slot = 3 * g + j
            s, p = ahead
            if j < 2:
                ahead = products(slot + 1)
            if masked:
                at = lax.broadcasted_iota(jnp.int32, (tile_len, tile_len), 0)
                frame_at = frame + kind * outer
                row_at = jnp.clip(row + kind * inner + (1 - kind) * outer, 0, rows - 1)
                col_at = jnp.clip(col + (1 - kind) * inner, 0, cols - 1)
                count = counts_ref[frame_at, row_at * cols + col_at]
                count = jnp.where(has_inner(kind, inner), count, 0)
                s = jnp.where(at < count, s, -1e30)
            top = jnp.max(jnp.max(groups(s), axis=0), axis=0, keepdims=True) * c2
            e = jnp.exp2(s * c2 - top)
            s_scr[slot] = e
            p_scr[slot] = p
            m_row[slot, 0:1, :] = top
            l_row[slot, 0:1, :] = jnp.sum(jnp.sum(groups(e), axis=0), axis=0, keepdims=True)
            d_row[slot, 0:1, :] = jnp.sum(jnp.sum(groups(e * p), axis=0), axis=0, keepdims=True)

    def query_pass(kind, pair):
        m_row[...] = jnp.full(m_row.shape, -1e30, jnp.float32)
        l_row[...] = jnp.zeros_like(l_row)
        d_row[...] = jnp.zeros_like(d_row)
        qacc[...] = jnp.zeros_like(qacc)

        @pl.loop(0, 3)
        def _(g):
            outer = step_of(g)

            @pl.when(has_outer(kind, outer))
            def _():
                await_group(big, kind, pair, 0, g)
                inner_at, inner_size = inner_pos(kind)
                frame_at = frame + kind * outer
                lowest = row + (1 - kind) * outer + kind
                partial = (frame_at == frames - 1) | (lowest >= rows - 1)
                partial = partial | (inner_at == 0) | (inner_at == inner_size - 1)

                @pl.when(partial)
                def _():
                    query_group(kind, pair, g, True)

                @pl.when(jnp.logical_not(partial))
                def _():
                    query_group(kind, pair, g, False)

        tops = [m_row[slot, 0:1, :] for slot in range(9)]
        top = functools.reduce(jnp.maximum, tops)
        parts = [jnp.exp2(t - top) for t in tops]
        total = sum(parts[slot] * l_row[slot, 0:1, :] for slot in range(9))
        inv = 1.0 / total
        dot_row = sum(parts[slot] * d_row[slot, 0:1, :] for slot in range(9)) * inv
        for slot in range(9):
            m_row[slot, 0:1, :] = parts[slot] * inv
        stats[kind, pair, 0, 0:1, :] = top + jnp.log(total) * LOG2E
        stats[kind, pair, 0, 1:2, :] = dot_row

        @pl.loop(0, 3)
        def _(g):
            @pl.when(has_outer(kind, step_of(g)))
            def _():
                total_q = qacc[...]
                for j in range(3):
                    slot = 3 * g + j
                    ds = s_scr[slot] * m_row[slot, 0:1, :] * (p_scr[slot] - dot_row)
                    total_q = total_q + dot_tn(held[kind, pair, 0, slot, :, 0:hd], ds.astype(jnp.bfloat16))
                qacc[...] = total_q

        qres[kind, pair] = (qacc[...].T * scale).astype(jnp.bfloat16)
        own(small, kind, pair, 0)

    def key_slots(kind, pair, slots):
        keys = held[kind, pair, 0, 0, :, 0:hd]
        values = held[kind, pair, 0, 0, :, hd:]

        def products(slot):
            query = held[kind, pair, 1, slot, :, 0:hd]
            grad = held[kind, pair, 1, slot, :, hd:]
            return dot_nt(keys, query), dot_nt(values, grad)

        def weights(slot, s, p):
            soft = jnp.exp2(s * c2 - stats[kind, pair, slot, 0:1, :])
            ds = soft * (p - stats[kind, pair, slot, 1:2, :])
            return soft.astype(jnp.bfloat16), ds.astype(jnp.bfloat16)

        ahead = products(slots[0])
        v, k = vacc[kind, pair], kacc[kind, pair]
        for at, slot in enumerate(slots):
            s, p = ahead
            if at + 1 < len(slots):
                ahead = products(slots[at + 1])
            soft, ds = weights(slot, s, p)
            v = v + dot_nn(soft, held[kind, pair, 1, slot, :, hd:])
            k = k + dot_nn(ds, held[kind, pair, 1, slot, :, 0:hd])
        vacc[kind, pair] = v
        kacc[kind, pair] = k

    def key_outer(kind, pair, j):
        has = (has_outer(kind, -1), has_outer(kind, 1))
        for g in (1, 2):

            @pl.when(has[g - 1])
            def _():
                device = outer_id(kind, step_of(g))
                big(kind, pair, 1, 0, 3 * g + j, device).wait_recv()
                small(kind, pair, 0, 0, 3 * g + j, device).wait_recv()

        @pl.when(has[0] & has[1])
        def _():
            key_slots(kind, pair, (3 + j, 6 + j))

        @pl.when(jnp.logical_not(has[0] & has[1]))
        def _():
            key_slots(kind, pair, (6 + j - 3 * has[0].astype(jnp.int32),))

    @pl.loop(0, pairs)
    def _(pair):
        own_chunk(pair + pairs)

        @pl.when(pair >= 1)
        def _():
            pump_chunk(0, pair + pairs - 1)
            for kind in (0, 1):
                pump(small, kind, pair - 1, 0)

        @pl.when(pair == 2)
        def _():
            pump_chunk(1, jnp.int32(pairs))

        @pl.loop(0, 2)
        def _(at):
            query_pass(first_kind + at * (1 - 2 * first_kind), pair)

        @pl.when(pair == 0)
        def _():
            relay_chunk(jnp.int32(2))

    pump_chunk(1, jnp.int32(pairs + 1))
    pump_chunk(0, jnp.int32(2 * pairs - 1))
    relay_chunk(jnp.int32(pairs))

    def place(res, out, pair):
        plane, across = res[0, pair], res[1, pair]
        at = 2 * pair * hd
        out[:, at : at + hd] = jnp.where(flags[pair], across, plane)
        out[:, at + hd : at + 2 * hd] = jnp.where(flags[pair], plane, across)

    order = (
        (0, 0, 0), (0, 0, 1), (0, 0, 2), (1, 0, 0), (1, 0, 1), (1, 0, 2),
        (0, 1, 0), (1, 1, 0), (0, 1, 1), (0, 1, 2),
        (0, 2, 0), (1, 2, 0),
        (1, 1, 1), (1, 1, 2),
        (0, 2, 1), (0, 2, 2), (1, 2, 1), (1, 2, 2),
    )

    @pl.loop(0, len(order))
    def _(step):
        def pick(part):
            found = jnp.int32(0)
            for at, entry in enumerate(order):
                if entry[part]:
                    found = found + entry[part] * (step == at).astype(jnp.int32)
            return found

        later, pair, j = pick(0), pick(1), pick(2)
        kind = first_kind + later * (1 - 2 * first_kind)

        @pl.when(step == 6)
        def _():
            for kind in (0, 1):
                pump(small, kind, pairs - 1, 0)

        @pl.when(step == 8)
        def _():
            pump_chunk(1, jnp.int32(2 * pairs - 1))
            relay_chunk(jnp.int32(2 * pairs - 2))

        @pl.when(step == 14)
        def _():
            for done in range(pairs - 1):
                place(kres, dk_ref, done)
                place(vres, dv_ref, done)
            for done in range(pairs):
                place(qres, dq_ref, done)

        @pl.when(j == 0)
        def _():
            kacc[kind, pair] = jnp.zeros(kacc.shape[2:], kacc.dtype)
            vacc[kind, pair] = jnp.zeros(vacc.shape[2:], vacc.dtype)
            key_slots(kind, pair, (0, 1, 2))

        @pl.when(has_inner(kind, step_of(j)))
        def _():
            key_outer(kind, pair, j)

        @pl.when(j == 2)
        def _():
            kres[kind, pair] = jnp.where(live, kacc[kind, pair] * scale, 0.0).astype(jnp.bfloat16)
            vres[kind, pair] = jnp.where(live, vacc[kind, pair], 0.0).astype(jnp.bfloat16)

    place(kres, dk_ref, pairs - 1)
    place(vres, dv_ref, pairs - 1)

    @pl.loop(0, pairs)
    def _(pair):
        for kind in (0, 1):
            drain(big, kind, pair, 0)
            drain(big, kind, pair, 1)
            drain(small, kind, pair, 0)
        for part in (0, 1):
            for_relays(pair, part, lambda copy, *_: copy.wait_send())


def write_out(dq, dk, dv, dq_out, dk_out, dv_out, sem):
    copies = [
        pltpu.make_async_copy(src, dst, sem.at[at])
        for at, (src, dst) in enumerate(((dq, dq_out), (dk, dk_out), (dv, dv_out)))
    ]
    for copy in copies:
        copy.start()
    for copy in copies:
        copy.wait()


def solution(mesh):
    frames = mesh.shape["frame"]
    cols = NCT
    rows = mesh.shape["tile"] // cols

    def local(queries, key_rows, value_rows, grad_rows, offsets, counts):
        tile_len, width = queries.shape[2:]
        heads = offsets.shape[0]
        pairs = heads // 2
        hd = width // heads
        vmem = pl.BlockSpec(memory_space=pltpu.VMEM)
        hbm = pl.BlockSpec(memory_space=pltpu.HBM)
        out = jax.ShapeDtypeStruct((tile_len, width), jnp.bfloat16)
        f32 = jnp.float32
        low = jnp.bfloat16
        steps = jnp.transpose(offsets, (0, 2, 1))
        results = pl.pallas_call(
            functools.partial(kernel, frames, rows, cols),
            out_shape=(out, out, out),
            in_specs=[hbm] * 6,
            out_specs=(vmem, vmem, vmem),
            scratch_shapes=[
                pltpu.SMEM(steps.shape, jnp.int32),
                pltpu.SMEM(counts.shape, jnp.int32),
                pltpu.VMEM((tile_len, width), low),
                pltpu.VMEM((tile_len, width), low),
                pltpu.VMEM((tile_len, width), low),
                pltpu.VMEM(grad_rows.shape[2:], low),
                pltpu.VMEM((2, pairs, 2, 9, tile_len, 2 * hd), low),
                pltpu.VMEM((2, pairs, 9, 8, tile_len), f32),
                pltpu.VMEM((9, tile_len, tile_len), f32),
                pltpu.VMEM((9, tile_len, tile_len), f32),
                pltpu.VMEM((tile_len, width), low),
                pltpu.VMEM((9, 8, tile_len), f32),
                pltpu.VMEM((9, 8, tile_len), f32),
                pltpu.VMEM((9, 8, tile_len), f32),
                pltpu.VMEM((hd, tile_len), f32),
                pltpu.VMEM((2, pairs, tile_len, hd), f32),
                pltpu.VMEM((2, pairs, tile_len, hd), f32),
                pltpu.VMEM((2, pairs, tile_len, hd), low),
                pltpu.VMEM((2, pairs, tile_len, hd), low),
                pltpu.VMEM((2, pairs, tile_len, hd), low),
                pltpu.SemaphoreType.DMA((2, pairs, 2, 9)),
                pltpu.SemaphoreType.DMA((2, pairs, 2, 9)),
                pltpu.SemaphoreType.DMA((2, pairs, 9)),
                pltpu.SemaphoreType.DMA((2, pairs, 9)),
                pltpu.SemaphoreType.DMA,
                pltpu.SemaphoreType.DMA,
                pltpu.SemaphoreType.DMA((6,)),
            ],
            compiler_params=pltpu.CompilerParams(
                collective_id=0, has_side_effects=True, vmem_limit_bytes=48 * 1024 * 1024
            ),
        )(
            *(
                pltpu.with_memory_space_constraint(array, pltpu.HBM)
                for array in (steps, counts, queries[0, 0], key_rows[0, 0], value_rows[0, 0], grad_rows[0, 0])
            ),
        )
        dq, dk, dv = pl.pallas_call(
            write_out,
            out_shape=(out, out, out),
            in_specs=[vmem, vmem, vmem],
            out_specs=(hbm, hbm, hbm),
            scratch_shapes=[
                pltpu.SemaphoreType.DMA((3,)),
            ],
            compiler_params=pltpu.CompilerParams(vmem_limit_bytes=8 * 1024 * 1024),
        )(*results)
        return dq[None, None], dk[None, None], dv[None, None]

    return jax.shard_map(
        local,
        mesh=mesh,
        in_specs=(
            P("frame", "tile", None, "section"),
            P("frame", "tile", None, "section"),
            P("frame", "tile", None, "section"),
            P("frame", "tile", "section", None),
            P("section", None, None),
            P(),
        ),
        out_specs=(
            P("frame", "tile", None, "section"),
            P("frame", "tile", None, "section"),
            P("frame", "tile", None, "section"),
        ),
        check_vma=False,
    )
```

```python
import functools
import math

import jax
import jax.numpy as jnp
from jax import lax
from jax.experimental import pallas as pl
from jax.experimental.pallas import tpu as pltpu
from jax.sharding import PartitionSpec as P

NCT = 4
MESH = pl.DeviceIdType.MESH
LOG2E = 1.4426950408889634
RELAY = 2


def dot_nt(a, b):
    return lax.dot_general(a, b, (((1,), (1,)), ((), ())), preferred_element_type=jnp.float32)


def dot_nn(a, b):
    return lax.dot_general(a, b, (((1,), (0,)), ((), ())), preferred_element_type=jnp.float32)


def dot_tn(a, b):
    return lax.dot_general(a, b, (((0,), (0,)), ((), ())), preferred_element_type=jnp.float32)


def spans_frames(offs_ref, pair):
    seen = jnp.int32(0)
    for o in range(offs_ref.shape[2]):
        step = offs_ref[2 * pair, 0, o]
        seen = seen + step * step
    return seen > 0


def step_of(code):
    return (code * (3 * code - 5)) // 2


def kernel(
    frames,
    rows,
    cols,
    offs_hbm,
    counts_hbm,
    q_hbm,
    k_hbm,
    v_hbm,
    g_hbm,
    dq_ref,
    dk_ref,
    dv_ref,
    offs_ref,
    counts_ref,
    q_ref,
    k_ref,
    v_ref,
    g_ref,
    held,
    stats,
    s_scr,
    p_scr,
    gbuf,
    m_row,
    l_row,
    d_row,
    qacc,
    kacc,
    vacc,
    qres,
    kres,
    vres,
    send_sem,
    recv_sem,
    stat_send,
    stat_recv,
    g_send,
    g_recv,
    in_sem,
):
    loads = [
        pltpu.make_async_copy(src, dst, in_sem.at[at])
        for at, (src, dst) in enumerate(
            (
                (offs_hbm, offs_ref),
                (k_hbm, k_ref),
                (v_hbm, v_ref),
                (g_hbm, g_ref),
                (q_hbm, q_ref),
                (counts_hbm, counts_ref),
            )
        )
    ]
    for load in loads:
        load.start()
    tile_len, width = q_ref.shape
    pairs = held.shape[1]
    hd = held.shape[4] // 2
    half = g_ref.shape[0]
    scale = 1.0 / math.sqrt(hd)
    c2 = scale * LOG2E
    frame = lax.axis_index("frame")
    tile = lax.axis_index("tile")
    section = lax.axis_index("section")
    row = tile // cols
    col = tile % cols

    def inner_pos(kind):
        return col + kind * (row - col), cols + kind * (rows - cols)

    def outer_pos(kind):
        return row + kind * (frame - row), rows + kind * (frames - rows)

    def has_inner(kind, step):
        pos, size = inner_pos(kind)
        return (pos + step >= 0) & (pos + step < size)

    def has_outer(kind, step):
        pos, size = outer_pos(kind)
        return (pos + step >= 0) & (pos + step < size)

    def inner_id(kind, step):
        return {"tile": tile + step * (1 + kind * (cols - 1))}

    def outer_id(kind, step):
        return {"tile": tile + step * (1 - kind) * cols, "frame": frame + step * kind}

    def big(kind, pair, part, src, dst, device, at=None):
        return pltpu.make_async_remote_copy(
            src_ref=held.at[kind, pair, part, src],
            dst_ref=held.at[kind, pair, part, dst],
            send_sem=send_sem.at[kind, pair, part, dst if at is None else at],
            recv_sem=recv_sem.at[kind, pair, part, dst],
            device_id=device,
            device_id_type=MESH,
        )

    def small(kind, pair, part, src, dst, device, at=None):
        return pltpu.make_async_remote_copy(
            src_ref=stats.at[kind, pair, src],
            dst_ref=stats.at[kind, pair, dst],
            send_sem=stat_send.at[kind, pair, dst],
            recv_sem=stat_recv.at[kind, pair, dst],
            device_id=device,
            device_id_type=MESH,
        )

    mid = frames // 2 - 1
    via_up = frames - 1 if RELAY == 1 else 0
    via_down = frames - 1 - via_up

    def outer_copy(copy, kind, pair, part, code, step, j):
        dst = 3 * code + j
        device = outer_id(kind, step)
        if RELAY and copy is big and kind == 1 and j:
            aside = (part * pairs + pair < 2 * pairs - j).astype(jnp.int32)
            if step == 1:
                crossing = (frame == mid).astype(jnp.int32) * aside
                device["frame"] = frame + 1 + crossing * (via_up - mid - 1)
                land = dst + crossing * (3 if via_up else 0)
            else:
                crossing = (frame == mid + 1).astype(jnp.int32) * aside
                device["frame"] = frame - 1 + crossing * (via_down - mid)
                land = dst - crossing * (0 if via_down else 3)
            return copy(kind, pair, part, j, land, device, dst)
        return copy(kind, pair, part, j, dst, device)

    def relay_copy(pair, part, j, first):
        up = (via_up == 0) == first
        src = (3 if first else 6) + j
        return big(1, pair, part, src, (3 if up else 6) + j, {"frame": mid + 1 if up else mid}, (6 if first else 3) + j)

    def for_relays(pair, part, act):
        if not RELAY:
            return
        for first in (True, False):
            for j, from_step in ((1, -1), (2, 1)):
                go = has_inner(1, from_step) & (frame == (0 if first else frames - 1))
                go = go & (part * pairs + pair < 2 * pairs - j)

                @pl.when(go)
                def _():
                    act(relay_copy(pair, part, j, first), pair, part, (3 if first else 6) + j)

    def forward(copy, pair, part, slot):
        big(1, pair, part, 0, slot, {"frame": mid}).wait_recv()
        copy.start()

    def relay_chunk(chunk):
        for_relays(lax.rem(chunk, pairs), chunk // pairs, forward)

    def own(copy, kind, pair, part):
        for code, step in ((1, 1), (2, -1)):

            @pl.when(has_inner(kind, step))
            def _():
                copy(kind, pair, part, 0, code, inner_id(kind, step)).start()

            @pl.when(has_outer(kind, step))
            def _():
                outer_copy(copy, kind, pair, part, code, step, 0).start()

    def pump(copy, kind, pair, part):
        for j, from_step in ((1, -1), (2, 1)):

            @pl.when(has_inner(kind, from_step))
            def _():
                copy(kind, pair, part, 0, j, inner_id(kind, from_step)).wait_recv()
                for code, step in ((1, 1), (2, -1)):

                    @pl.when(has_outer(kind, step))
                    def _():
                        outer_copy(copy, kind, pair, part, code, step, j).start()

    def drain(copy, kind, pair, part):
        for code, step in ((1, 1), (2, -1)):

            @pl.when(has_inner(kind, step))
            def _():
                copy(kind, pair, part, 0, code, inner_id(kind, step)).wait_send()

            @pl.when(has_outer(kind, step))
            def _():
                outer_copy(copy, kind, pair, part, code, step, 0).wait_send()
                for j, from_step in ((1, -1), (2, 1)):

                    @pl.when(has_inner(kind, from_step))
                    def _():
                        outer_copy(copy, kind, pair, part, code, step, j).wait_send()

    def own_chunk(chunk):
        for kind in (0, 1):
            own(big, kind, lax.rem(chunk, pairs), chunk // pairs)

    def pump_chunk(kind, chunk):
        pump(big, kind, lax.rem(chunk, pairs), chunk // pairs)

    barrier = pltpu.get_barrier_semaphore()
    partner = {"section": 1 - section}
    pl.semaphore_signal(barrier, inc=1, device_id=partner, device_id_type=MESH)
    expected = jnp.int32(1)
    for make, has in (
        (functools.partial(inner_id, 0), functools.partial(has_inner, 0)),
        (functools.partial(outer_id, 0), functools.partial(has_outer, 0)),
        (functools.partial(outer_id, 1), functools.partial(has_outer, 1)),
    ):
        for step in (1, -1):
            expected = expected + has(step).astype(jnp.int32)

            @pl.when(has(step))
            def _():
                pl.semaphore_signal(barrier, inc=1, device_id=make(step), device_id_type=MESH)

    if RELAY:
        for ends, others in (((0, frames - 1), (mid, mid + 1)), ((mid, mid + 1), (0, frames - 1))):
            inside = (frame == ends[0]) | (frame == ends[1])
            expected = expected + 2 * inside.astype(jnp.int32)

            @pl.when(inside)
            def _():
                for other in others:
                    pl.semaphore_signal(barrier, inc=1, device_id={"frame": other}, device_id_type=MESH)

    loads[0].wait()
    flags = [spans_frames(offs_ref, pair) for pair in range(pairs)]

    def head(ref, h):
        return ref[:, h * hd : (h + 1) * hd]

    def pack_keys(pair):
        for at, ref in ((0, k_ref), (1, v_ref)):
            even, odd = head(ref, 2 * pair), head(ref, 2 * pair + 1)
            lanes = slice(at * hd, (at + 1) * hd)
            held[0, pair, 0, 0, :, lanes] = jnp.where(flags[pair], odd, even)
            held[1, pair, 0, 0, :, lanes] = jnp.where(flags[pair], even, odd)

    loads[1].wait()
    loads[2].wait()
    pack_keys(0)
    loads[3].wait()
    pl.semaphore_wait(barrier, expected)

    swap = pltpu.make_async_remote_copy(
        src_ref=g_ref.at[:, pl.ds(pl.multiple_of((1 - section) * width, 128), width)],
        dst_ref=gbuf.at[pl.ds(pl.multiple_of(section * half, 16), half)],
        send_sem=g_send,
        recv_sem=g_recv,
        device_id=partner,
        device_id_type=MESH,
    )
    swap.start()
    own_chunk(0)
    for pair in range(1, pairs):
        pack_keys(pair)
    for chunk in range(1, pairs):
        own_chunk(chunk)

    for kind in (0, 1):
        for j, from_step in ((1, -1), (2, 1)):

            @pl.when(jnp.logical_not(has_inner(kind, from_step)))
            def _():
                @pl.loop(0, pairs)
                def _(pair):
                    @pl.loop(0, 3)
                    def _(g):
                        held[kind, pair, 0, 3 * g + j] = jnp.zeros(held.shape[4:], held.dtype)
                        held[kind, pair, 1, 3 * g + j] = jnp.zeros(held.shape[4:], held.dtype)
                        stats[kind, pair, 3 * g + j] = jnp.zeros(stats.shape[3:], stats.dtype)

    gbuf[pl.ds(pl.multiple_of(section * half, 16), half), :] = g_ref[
        :, pl.ds(pl.multiple_of(section * width, 128), width)
    ]
    loads[4].wait()
    loads[5].wait()
    swap.wait()
    own_count = counts_ref[frame, tile]
    live = lax.broadcasted_iota(jnp.int32, (tile_len, hd), 0) < own_count
    for pair in range(pairs):
        even, odd = head(q_ref, 2 * pair), head(q_ref, 2 * pair + 1)
        held[0, pair, 1, 0, :, 0:hd] = jnp.where(flags[pair], odd, even)
        held[1, pair, 1, 0, :, 0:hd] = jnp.where(flags[pair], even, odd)
        even = jnp.where(live, head(gbuf, 2 * pair).astype(jnp.float32), 0.0).astype(jnp.bfloat16)
        odd = jnp.where(live, head(gbuf, 2 * pair + 1).astype(jnp.float32), 0.0).astype(jnp.bfloat16)
        held[0, pair, 1, 0, :, hd:] = jnp.where(flags[pair], odd, even)
        held[1, pair, 1, 0, :, hd:] = jnp.where(flags[pair], even, odd)

    for chunk in range(pairs):
        for kind in (0, 1):
            pump_chunk(kind, chunk)
    relay_chunk(0)
    relay_chunk(1)

    crossing = (frame == mid) | (frame == mid + 1)
    first_kind = 1 - crossing.astype(jnp.int32)

    def groups(x):
        return x.reshape(x.shape[0] // 8, 8, x.shape[1])

    def await_group(copy, kind, pair, part, g):
        @pl.when(g > 0)
        def _():
            for j, from_step in ((0, 0), (1, -1), (2, 1)):

                @pl.when(has_inner(kind, from_step))
                def _():
                    copy(kind, pair, part, 0, 3 * g + j, outer_id(kind, step_of(g))).wait_recv()

    def query_group(kind, pair, g, masked):
        query = held[kind, pair, 1, 0, :, 0:hd]
        grad = held[kind, pair, 1, 0, :, hd:]
        outer = step_of(g)

        def products(slot):
            return dot_nt(held[kind, pair, 0, slot, :, 0:hd], query), dot_nt(held[kind, pair, 0, slot, :, hd:], grad)

        ahead = products(3 * g)
        for j, inner in ((0, 0), (1, -1), (2, 1)):
            slot = 3 * g + j
            s, p = ahead
            if j < 2:
                ahead = products(slot + 1)
            if masked:
                at = lax.broadcasted_iota(jnp.int32, (tile_len, tile_len), 0)
                frame_at = frame + kind * outer
                row_at = jnp.clip(row + kind * inner + (1 - kind) * outer, 0, rows - 1)
                col_at = jnp.clip(col + (1 - kind) * inner, 0, cols - 1)
                count = counts_ref[frame_at, row_at * cols + col_at]
                count = jnp.where(has_inner(kind, inner), count, 0)
                s = jnp.where(at < count, s, -1e30)
            top = jnp.max(jnp.max(groups(s), axis=0), axis=0, keepdims=True) * c2
            e = jnp.exp2(s * c2 - top)
            s_scr[slot] = e
            p_scr[slot] = p
            m_row[slot, 0:1, :] = top
            l_row[slot, 0:1, :] = jnp.sum(jnp.sum(groups(e), axis=0), axis=0, keepdims=True)
            d_row[slot, 0:1, :] = jnp.sum(jnp.sum(groups(e * p), axis=0), axis=0, keepdims=True)

    def query_pass(kind, pair):
        m_row[...] = jnp.full(m_row.shape, -1e30, jnp.float32)
        l_row[...] = jnp.zeros_like(l_row)
        d_row[...] = jnp.zeros_like(d_row)
        qacc[...] = jnp.zeros_like(qacc)

        @pl.loop(0, 3)
        def _(g):
            outer = step_of(g)

            @pl.when(has_outer(kind, outer))
            def _():
                await_group(big, kind, pair, 0, g)
                inner_at, inner_size = inner_pos(kind)
                frame_at = frame + kind * outer
                lowest = row + (1 - kind) * outer + kind
                partial = (frame_at == frames - 1) | (lowest >= rows - 1)
                partial = partial | (inner_at == 0) | (inner_at == inner_size - 1)

                @pl.when(partial)
                def _():
                    query_group(kind, pair, g, True)

                @pl.when(jnp.logical_not(partial))
                def _():
                    query_group(kind, pair, g, False)

        tops = [m_row[slot, 0:1, :] for slot in range(9)]
        top = functools.reduce(jnp.maximum, tops)
        parts = [jnp.exp2(t - top) for t in tops]
        total = sum(parts[slot] * l_row[slot, 0:1, :] for slot in range(9))
        inv = 1.0 / total
        dot_row = sum(parts[slot] * d_row[slot, 0:1, :] for slot in range(9)) * inv
        for slot in range(9):
            m_row[slot, 0:1, :] = parts[slot] * inv
        stats[kind, pair, 0, 0:1, :] = top + jnp.log(total) * LOG2E
        stats[kind, pair, 0, 1:2, :] = dot_row

        @pl.loop(0, 3)
        def _(g):
            @pl.when(has_outer(kind, step_of(g)))
            def _():
                total_q = qacc[...]
                for j in range(3):
                    slot = 3 * g + j
                    ds = s_scr[slot] * m_row[slot, 0:1, :] * (p_scr[slot] - dot_row)
                    total_q = total_q + dot_tn(held[kind, pair, 0, slot, :, 0:hd], ds.astype(jnp.bfloat16))
                qacc[...] = total_q

        qres[kind, pair] = (qacc[...].T * scale).astype(jnp.bfloat16)
        own(small, kind, pair, 0)

    def key_slots(kind, pair, slots):
        keys = held[kind, pair, 0, 0, :, 0:hd]
        values = held[kind, pair, 0, 0, :, hd:]

        def products(slot):
            query = held[kind, pair, 1, slot, :, 0:hd]
            grad = held[kind, pair, 1, slot, :, hd:]
            return dot_nt(keys, query), dot_nt(values, grad)

        def weights(slot, s, p):
            soft = jnp.exp2(s * c2 - stats[kind, pair, slot, 0:1, :])
            ds = soft * (p - stats[kind, pair, slot, 1:2, :])
            return soft.astype(jnp.bfloat16), ds.astype(jnp.bfloat16)

        ahead = products(slots[0])
        v, k = vacc[kind, pair], kacc[kind, pair]
        for at, slot in enumerate(slots):
            s, p = ahead
            if at + 1 < len(slots):
                ahead = products(slots[at + 1])
            soft, ds = weights(slot, s, p)
            v = v + dot_nn(soft, held[kind, pair, 1, slot, :, hd:])
            k = k + dot_nn(ds, held[kind, pair, 1, slot, :, 0:hd])
        vacc[kind, pair] = v
        kacc[kind, pair] = k

    def key_outer(kind, pair, j):
        has = (has_outer(kind, -1), has_outer(kind, 1))
        for g in (1, 2):

            @pl.when(has[g - 1])
            def _():
                device = outer_id(kind, step_of(g))
                big(kind, pair, 1, 0, 3 * g + j, device).wait_recv()
                small(kind, pair, 0, 0, 3 * g + j, device).wait_recv()

        @pl.when(has[0] & has[1])
        def _():
            key_slots(kind, pair, (3 + j, 6 + j))

        @pl.when(jnp.logical_not(has[0] & has[1]))
        def _():
            key_slots(kind, pair, (6 + j - 3 * has[0].astype(jnp.int32),))

    @pl.loop(0, pairs)
    def _(pair):
        @pl.when(pair != 1)
        def _():
            own_chunk(pair + pairs)

        @pl.when(pair >= 1)
        def _():
            pump_chunk(0, pair + pairs - 1)
            for kind in (0, 1):
                pump(small, kind, pair - 1, 0)

        @pl.when(pair == 1)
        def _():
            own_chunk(pair + pairs)

        @pl.when(pair == 2)
        def _():
            pump_chunk(1, jnp.int32(pairs))

        @pl.loop(0, 2)
        def _(at):
            query_pass(first_kind + at * (1 - 2 * first_kind), pair)

        @pl.when(pair == 0)
        def _():
            relay_chunk(jnp.int32(2))

    pump_chunk(0, jnp.int32(2 * pairs - 1))
    relay_chunk(jnp.int32(pairs))

    def place(res, out, pair):
        plane, across = res[0, pair], res[1, pair]
        at = 2 * pair * hd
        out[:, at : at + hd] = jnp.where(flags[pair], across, plane)
        out[:, at + hd : at + 2 * hd] = jnp.where(flags[pair], plane, across)

    def finish(pair, last):
        for kind in (0, 1):
            if not last:
                drain(big, kind, pair, 0)
            drain(big, kind, pair, 1)
            drain(small, kind, pair, 0)
        for part in (0, 1):
            if part or not last:
                for_relays(pair, part, lambda copy, *_: copy.wait_send())

    order = (
        (0, 0, 0), (0, 0, 1), (0, 0, 2), (1, 0, 0), (1, 0, 1), (1, 0, 2),
        (0, 1, 0), (1, 1, 0),
        (0, 2, 0), (1, 2, 0),
        (0, 1, 1), (0, 1, 2), (1, 1, 1), (1, 1, 2),
        (0, 2, 1), (0, 2, 2), (1, 2, 1), (1, 2, 2),
    )

    @pl.loop(0, len(order))
    def _(step):
        def pick(part):
            found = jnp.int32(0)
            for at, entry in enumerate(order):
                if entry[part]:
                    found = found + entry[part] * (step == at).astype(jnp.int32)
            return found

        later, pair, j = pick(0), pick(1), pick(2)
        kind = first_kind + later * (1 - 2 * first_kind)

        @pl.when(step == 6)
        def _():
            for kind in (0, 1):
                pump(small, kind, pairs - 1, 0)
            pump_chunk(1, jnp.int32(pairs + 1))

        @pl.when(step == 8)
        def _():
            pump_chunk(1, jnp.int32(2 * pairs - 1))
            relay_chunk(jnp.int32(2 * pairs - 2))

        @pl.when(step == 14)
        def _():
            for done in range(pairs - 1):
                place(kres, dk_ref, done)
                place(vres, dv_ref, done)
            for done in range(pairs):
                place(qres, dq_ref, done)

            @pl.loop(0, pairs - 1)
            def _(done):
                finish(done, False)

            for kind in (0, 1):
                drain(big, kind, jnp.int32(pairs - 1), 0)
            for_relays(jnp.int32(pairs - 1), 0, lambda copy, *_: copy.wait_send())

        @pl.when(j == 0)
        def _():
            kacc[kind, pair] = jnp.zeros(kacc.shape[2:], kacc.dtype)
            vacc[kind, pair] = jnp.zeros(vacc.shape[2:], vacc.dtype)
            key_slots(kind, pair, (0, 1, 2))

        @pl.when(has_inner(kind, step_of(j)))
        def _():
            key_outer(kind, pair, j)

        @pl.when(j == 2)
        def _():
            kres[kind, pair] = jnp.where(live, kacc[kind, pair] * scale, 0.0).astype(jnp.bfloat16)
            vres[kind, pair] = jnp.where(live, vacc[kind, pair], 0.0).astype(jnp.bfloat16)

    place(kres, dk_ref, pairs - 1)
    place(vres, dv_ref, pairs - 1)

    finish(jnp.int32(pairs - 1), True)


def write_out(dq, dk, dv, dq_out, dk_out, dv_out, sem):
    copies = [
        pltpu.make_async_copy(src, dst, sem.at[at])
        for at, (src, dst) in enumerate(((dq, dq_out), (dk, dk_out), (dv, dv_out)))
    ]
    for copy in copies:
        copy.start()
    for copy in copies:
        copy.wait()


def solution(mesh):
    frames = mesh.shape["frame"]
    cols = NCT
    rows = mesh.shape["tile"] // cols

    def local(queries, key_rows, value_rows, grad_rows, offsets, counts):
        tile_len, width = queries.shape[2:]
        heads = offsets.shape[0]
        pairs = heads // 2
        hd = width // heads
        vmem = pl.BlockSpec(memory_space=pltpu.VMEM)
        hbm = pl.BlockSpec(memory_space=pltpu.HBM)
        out = jax.ShapeDtypeStruct((tile_len, width), jnp.bfloat16)
        f32 = jnp.float32
        low = jnp.bfloat16
        steps = jnp.transpose(offsets, (0, 2, 1))
        results = pl.pallas_call(
            functools.partial(kernel, frames, rows, cols),
            out_shape=(out, out, out),
            in_specs=[hbm] * 6,
            out_specs=(vmem, vmem, vmem),
            scratch_shapes=[
                pltpu.SMEM(steps.shape, jnp.int32),
                pltpu.SMEM(counts.shape, jnp.int32),
                pltpu.VMEM((tile_len, width), low),
                pltpu.VMEM((tile_len, width), low),
                pltpu.VMEM((tile_len, width), low),
                pltpu.VMEM(grad_rows.shape[2:], low),
                pltpu.VMEM((2, pairs, 2, 9, tile_len, 2 * hd), low),
                pltpu.VMEM((2, pairs, 9, 8, tile_len), f32),
                pltpu.VMEM((9, tile_len, tile_len), f32),
                pltpu.VMEM((9, tile_len, tile_len), f32),
                pltpu.VMEM((tile_len, width), low),
                pltpu.VMEM((9, 8, tile_len), f32),
                pltpu.VMEM((9, 8, tile_len), f32),
                pltpu.VMEM((9, 8, tile_len), f32),
                pltpu.VMEM((hd, tile_len), f32),
                pltpu.VMEM((2, pairs, tile_len, hd), f32),
                pltpu.VMEM((2, pairs, tile_len, hd), f32),
                pltpu.VMEM((2, pairs, tile_len, hd), low),
                pltpu.VMEM((2, pairs, tile_len, hd), low),
                pltpu.VMEM((2, pairs, tile_len, hd), low),
                pltpu.SemaphoreType.DMA((2, pairs, 2, 9)),
                pltpu.SemaphoreType.DMA((2, pairs, 2, 9)),
                pltpu.SemaphoreType.DMA((2, pairs, 9)),
                pltpu.SemaphoreType.DMA((2, pairs, 9)),
                pltpu.SemaphoreType.DMA,
                pltpu.SemaphoreType.DMA,
                pltpu.SemaphoreType.DMA((6,)),
            ],
            compiler_params=pltpu.CompilerParams(
                collective_id=0, has_side_effects=True, vmem_limit_bytes=48 * 1024 * 1024
            ),
        )(
            *(
                pltpu.with_memory_space_constraint(array, pltpu.HBM)
                for array in (steps, counts, queries[0, 0], key_rows[0, 0], value_rows[0, 0], grad_rows[0, 0])
            ),
        )
        dq, dk, dv = pl.pallas_call(
            write_out,
            out_shape=(out, out, out),
            in_specs=[vmem, vmem, vmem],
            out_specs=(hbm, hbm, hbm),
            scratch_shapes=[
                pltpu.SemaphoreType.DMA((3,)),
            ],
            compiler_params=pltpu.CompilerParams(vmem_limit_bytes=8 * 1024 * 1024),
        )(*results)
        return dq[None, None], dk[None, None], dv[None, None]

    return jax.shard_map(
        local,
        mesh=mesh,
        in_specs=(
            P("frame", "tile", None, "section"),
            P("frame", "tile", None, "section"),
            P("frame", "tile", None, "section"),
            P("frame", "tile", "section", None),
            P("section", None, None),
            P(),
        ),
        out_specs=(
            P("frame", "tile", None, "section"),
            P("frame", "tile", None, "section"),
            P("frame", "tile", None, "section"),
        ),
        check_vma=False,
    )
```
